768 devices in a mesh: cluster: 24 (over z, core), member: 32 (over x, y).
Axes of the slice: x: 4, y: 8, z: 12, core: 2. Of those that a mesh axis runs over, the one named last changes fastest.
Arguments:
- dual_load: float32 [24, 32, 64, 2, 1024], P('cluster', 'member'), may hold values from -110 to 110
- dual_operator: bfloat16 [2048, 2048], replicated, may hold values from -1.5859375 to 3.5859375, as said below
- index_map: int32 [24, 32, 2048], P('cluster', 'member'), may hold values from 0 to 2047, as said below
- stiffness: float32 [24, 32], P('cluster', 'member'), may hold values from 1 to 10
- coarse_basis: float32 [24, 32, 6, 2048], P('cluster', 'member'), may hold values from -2.5 to 2.5
- dirichlet_blocks: bfloat16 [24, 32, 16, 128, 128], P('cluster', 'member'), may hold values from -1 to 2.5, as said below
- coarse_inverse: float32 [144, 144], replicated, may hold values from -1 to 1, as said below
Outputs:
- multipliers: float32 [24, 32, 64, 2, 1024], P('cluster', 'member')
- residual: float32 [24, 32, 64, 2, 1024], P('cluster', 'member')
The draws below stay inside these ranges and needn't reach their ends.
Inputs may be any that keep to these rules, and one draw needn't show every extreme that they name: `dual_operator`: symmetric. `dirichlet_blocks`: each block is symmetric. `coarse_inverse`: symmetric. `index_map`: each subdomain's row names every position once.
All inputs are finite; a program needn't handle non-finite values.
Results may differ from the reference program's by a relative error of at most 0.0038.
Values sent between devices are 32-bit elements; how exact they have to be, the bound alone decides.
A program may use at most 64 MiB of HBM per device.

```python
import math
import jax
import jax.numpy as jnp
from jax import lax

DUAL = 2048
FACE = 1024
BLOCK = 128
NBLOCK = 16
MODES = 6
LOADS = 64
ITERS = 2
CLUSTERS = 24
MEMBERS = 32
COARSE = 144


def rough_draw(key, extent):
    return jax.random.truncated_normal(key, -4.0, 4.0, extent, jnp.float32)


def stiffness_draw(key):
    exponent = jax.random.uniform(jax.random.fold_in(key, 17), (CLUSTERS, MEMBERS), jnp.float32, 0.0, 1.0)
    return jnp.exp(exponent * math.log(10.0))


def one_order(subkey):
    return jax.random.permutation(subkey, DUAL)


def order_draw(key):
    keys = jax.random.split(jax.random.fold_in(key, 21), CLUSTERS * MEMBERS)
    orders = jax.vmap(one_order)(keys)
    return orders.astype(jnp.int32).reshape(CLUSTERS, MEMBERS, DUAL)


def shared_modes(key):
    return rough_draw(jax.random.fold_in(key, 23), (MODES, DUAL))


def basis_draw(key):
    orders = order_draw(key)
    aligned = jnp.take(shared_modes(key), orders, axis=1)
    aligned = jnp.moveaxis(aligned, 0, 2)
    own_part = rough_draw(jax.random.fold_in(key, 7), (CLUSTERS, MEMBERS, MODES, DUAL))
    return (0.8 * aligned + 0.6 * own_part) * (1.0 / math.sqrt(MODES))


def symmetric_draw(key, extent, order):
    sample = rough_draw(key, extent)
    return (sample + jnp.swapaxes(sample, -1, -2)) * (1.0 / math.sqrt(2.0 * order))


def draw_dual_operator(key, part):
    noise_part = symmetric_draw(jax.random.fold_in(key, 3), (DUAL, DUAL), DUAL)
    modes = shared_modes(key)
    strong_part = jnp.zeros((DUAL, DUAL), jnp.float32)
    for mode in range(MODES):
        strong_part = strong_part + modes[mode][:, None] * modes[mode][None, :]
    total = 1.5 * jnp.eye(DUAL, dtype=jnp.float32) + 0.5 * noise_part + 12.0 / DUAL * strong_part
    return total.astype(jnp.bfloat16)


def draw_index_map(key, part):
    return order_draw(key)


def draw_stiffness(key, part):
    return stiffness_draw(key)


def draw_dirichlet_blocks(key, part):
    noise_part = symmetric_draw(jax.random.fold_in(key, 5), (CLUSTERS, MEMBERS, NBLOCK, BLOCK, BLOCK), BLOCK)
    modulus = stiffness_draw(key).reshape(CLUSTERS, MEMBERS, 1, 1, 1)
    return (0.18 * modulus * (jnp.eye(BLOCK, dtype=jnp.float32) + 0.4 * noise_part)).astype(jnp.bfloat16)


def draw_coarse_inverse(key, part):
    magnitude = MODES / (MEMBERS * DUAL)
    noise_part = symmetric_draw(jax.random.fold_in(key, 11), (COARSE, COARSE), COARSE)
    return (jnp.eye(COARSE, dtype=jnp.float32) + 0.3 * noise_part) * magnitude


def draw_coarse_basis(key, part):
    return basis_draw(key)


def draw_dual_load(key, part):
    basis_rows = basis_draw(key)
    amplitude = rough_draw(jax.random.fold_in(key, 9), (CLUSTERS, MODES, LOADS))
    coarse = jnp.einsum('ckr,cmkl->cmrl', amplitude, basis_rows).reshape(CLUSTERS, MEMBERS, LOADS, 2, FACE)
    rough_part = rough_draw(jax.random.fold_in(key, 13), (CLUSTERS, MEMBERS, LOADS, 2, FACE))
    chain_ramp = jnp.linspace(0.6, 1.8, CLUSTERS * MEMBERS, dtype=jnp.float32).reshape(CLUSTERS, MEMBERS, 1, 1, 1)
    return (coarse + rough_part) * chain_ramp


def setup_inputs(seed: int = 0) -> dict:
    splits = jax.random.split(jax.random.key(seed), 8)
    return {
        "dual_load": draw_dual_load(jax.random.fold_in(splits[7], 71), 0),
        "dual_operator": draw_dual_operator(jax.random.fold_in(splits[7], 71), 0),
        "index_map": draw_index_map(jax.random.fold_in(splits[7], 71), 0),
        "stiffness": draw_stiffness(jax.random.fold_in(splits[7], 71), 0),
        "coarse_basis": draw_coarse_basis(jax.random.fold_in(splits[7], 71), 0),
        "dirichlet_blocks": draw_dirichlet_blocks(jax.random.fold_in(splits[7], 71), 0),
        "coarse_inverse": draw_coarse_inverse(jax.random.fold_in(splits[7], 71), 0),
    }


def assemble(part):
    zero = jnp.zeros_like(part[:1, :, 0])
    from_prev = jnp.concatenate([zero, part[:-1, :, 1]], axis=0)
    from_next = jnp.concatenate([part[1:, :, 0], zero], axis=0)
    return part + jnp.stack([from_prev, from_next], axis=2)


def reference(dual_load, dual_operator, index_map, stiffness, coarse_basis, dirichlet_blocks, coarse_inverse):
    exact_precision = lax.Precision.HIGHEST
    count = CLUSTERS * MEMBERS
    position = jnp.arange(count, dtype=jnp.int32)
    low_side = jnp.where(position > 0, 0.5, 1.0)
    high_side = jnp.where(position < count - 1, 0.5, 1.0)
    weights = jnp.stack([low_side, high_side], axis=1).astype(jnp.float32)[:, None, :, None]

    def inner(left, right):
        return jnp.sum(weights * left * right, axis=(0, 2, 3))

    def project(vector):
        folded = vector.reshape(CLUSTERS, MEMBERS, LOADS, DUAL)
        totals = jnp.einsum("cmrl,cmkl->rck", folded, coarse_basis, precision=exact_precision)
        totals = totals.reshape(LOADS, COARSE)
        amounts = jnp.dot(totals, coarse_inverse.T, precision=exact_precision)
        amounts = amounts.reshape(LOADS, CLUSTERS, MODES)
        spread = jnp.einsum("rck,cmkl->cmrl", amounts, coarse_basis, precision=exact_precision)
        return vector - assemble(spread.reshape(count, LOADS, 2, FACE))

    block_table = dirichlet_blocks.reshape(count, NBLOCK, BLOCK, BLOCK).astype(jnp.float32)
    operator_wide = dual_operator.astype(jnp.float32)

    def precondition(vector):
        scaled = (weights * vector).astype(jnp.bfloat16).reshape(count, LOADS, NBLOCK, BLOCK)
        blocked = jnp.einsum("srnj,snij->srni", scaled.astype(jnp.float32), block_table, precision=exact_precision)
        return assemble(weights * blocked.reshape(count, LOADS, 2, FACE))

    def subdomain_operator(inputs):
        flattened, ordering, modulus = inputs
        inverse = jnp.zeros((DUAL,), jnp.int32).at[ordering].set(jnp.arange(DUAL, dtype=jnp.int32))
        local_order = jnp.take(flattened, inverse, axis=1).astype(jnp.float32)
        product = jnp.dot(local_order, operator_wide, precision=exact_precision)
        return (1.0 / modulus) * jnp.take(product, ordering, axis=1)

    def apply(vector):
        rounded = vector.astype(jnp.bfloat16).reshape(count, LOADS, DUAL)
        local_image = lax.map(subdomain_operator, (rounded, index_map.reshape(count, DUAL).astype(jnp.int32), stiffness.reshape(count)))
        return assemble(local_image.reshape(count, LOADS, 2, FACE))

    residual = assemble(dual_load.reshape(count, LOADS, 2, FACE))
    multipliers = jnp.zeros_like(residual)
    direction = residual
    rho_prev = None
    for sweep in range(ITERS):
        projected = project(residual)
        search = project(precondition(projected))
        rho_now = inner(projected, search)
        if sweep == 0:
            direction = search
        else:
            direction = search + (rho_now / rho_prev)[None, :, None, None] * direction
        rho_prev = rho_now
        applied = apply(direction)
        step_size = (rho_now / inner(direction, applied))[None, :, None, None]
        multipliers = multipliers + step_size * direction
        residual = residual - step_size * applied
    return multipliers.reshape(dual_load.shape), residual.reshape(dual_load.shape)
```

```python
import functools
import jax
import jax.numpy as jnp
from jax import lax
from jax.experimental import pallas as pl
from jax.experimental.pallas import tpu as pltpu
from jax.sharding import PartitionSpec as P

MESH = pl.DeviceIdType.MESH
NY = 8
CORES = 2
GROUP = 8
SPAN = 32
LANES = 128
HALOS = 5
SUMS = 5
F32 = jnp.float32
BF16 = jnp.bfloat16


def nt(a, b):
    return lax.dot_general(a, b, (((1,), (1,)), ((), ())), preferred_element_type=F32)


def mm(a, b):
    return jnp.dot(a, b, preferred_element_type=F32)


def exact(a, b):
    return jnp.dot(a, b, precision=lax.Precision.HIGHEST, preferred_element_type=F32)


def split(v):
    high = v.astype(BF16)
    return high, (v - high.astype(F32)).astype(BF16)


def kernel(
    load_ref,
    basis_ref,
    blocks_ref,
    coarse_ref,
    index_ref,
    stiff_ref,
    oper_hbm,
    mult_out,
    resid_out,
    oper,
    own_basis,
    nbr_basis,
    span_f,
    span_h,
    span_l,
    coarse,
    inverse,
    halo,
    sent,
    resid,
    proj,
    search0,
    search1,
    image_q,
    temp,
    ybuf,
    xbuf,
    zbuf,
    oper_sem,
    basis_s,
    basis_r,
    halo_s,
    halo_r,
    y_s,
    y_r,
    x_s,
    x_r,
    z_s,
    z_r,
    c_s,
    c_r,
):
    loads, slots = load_ref.shape
    face = slots // 2
    chunks = slots // LANES
    modes = basis_ref.shape[0]
    nblock, block = blocks_ref.shape[:2]
    nz = zbuf.shape[2] - 2
    nx = xbuf.shape[1]
    ny = ybuf.shape[1]
    members = nx * ny
    c = lax.axis_index("cluster")
    m = lax.axis_index("member")
    z, core = c // CORES, lax.rem(c, CORES)
    x, y = m // ny, lax.rem(m, ny)
    chain = c * members + m
    last = nz * CORES * members - 1
    has_prev, has_next = chain > 0, chain < last
    first_m, last_m = m == 0, m == members - 1
    prev = (jnp.where(first_m, c - 1, c), jnp.where(first_m, members - 1, m - 1))
    nxt = (jnp.where(last_m, c + 1, c), jnp.where(last_m, 0, m + 1))
    y_peers = [(c, x * ny + lax.rem(y + i, ny)) for i in range(1, ny)]
    x_peers = [(c, lax.rem(x + i, nx) * ny + y) for i in range(1, nx)]
    z_peers = [(lax.rem(z + i, nz) * CORES + core, m) for i in range(1, nz)]
    partner = (z * CORES + 1 - core, m)

    def copy(src, dst, ss, rs, device):
        return pltpu.make_async_remote_copy(
            src_ref=src, dst_ref=dst, send_sem=ss, recv_sem=rs, device_id=device, device_id_type=MESH
        )

    def take(ref, sem):
        pltpu.make_async_copy(ref, ref, sem).wait()

    barrier = pltpu.get_barrier_semaphore()
    peers = y_peers + x_peers + z_peers + [partner]
    for peer in peers:
        pl.semaphore_signal(barrier, inc=1, device_id=peer, device_id_type=MESH)

    @pl.when(has_prev)
    def _():
        pl.semaphore_signal(barrier, inc=1, device_id=prev, device_id_type=MESH)

    @pl.when(has_next)
    def _():
        pl.semaphore_signal(barrier, inc=1, device_id=nxt, device_id_type=MESH)

    oper_copy = pltpu.make_async_copy(oper_hbm, oper, oper_sem)
    oper_copy.start()

    own_basis[...] = jnp.zeros_like(own_basis)
    for k in range(modes):
        own_basis[k : k + 1, :] = basis_ref[k]
    for k in range(SUMS):
        ybuf[k, y] = jnp.zeros((2 * GROUP, LANES), F32)
        for core_id in range(CORES):
            zbuf[k, core_id, 0] = jnp.zeros((2 * GROUP, LANES), F32)
            zbuf[k, core_id, nz + 1] = jnp.zeros((2 * GROUP, LANES), F32)

    @pl.when(jnp.logical_not(has_prev))
    def _():
        nbr_basis[0] = jnp.zeros((GROUP, face), F32)
        for k in range(HALOS):
            halo[k, 0] = jnp.zeros((loads, face), F32)

    @pl.when(jnp.logical_not(has_next))
    def _():
        nbr_basis[1] = jnp.zeros((GROUP, face), F32)
        for k in range(HALOS):
            halo[k, 1] = jnp.zeros((loads, face), F32)

    coarse_size = coarse_ref.shape[0]
    row = lax.broadcasted_iota(jnp.int32, (SPAN, coarse_size), 0)
    entry = lax.broadcasted_iota(jnp.int32, (SPAN, coarse_size), 1)
    wanted = modes * (c - 1 + (row >> 3)) + (row & 7)
    pick = jnp.where((wanted == entry) & ((row & 7) < modes) & (row < 3 * GROUP), 1.0, 0.0)
    total_rows = CORES * nz * GROUP
    entry = lax.broadcasted_iota(jnp.int32, (coarse_size, total_rows), 0)
    col = lax.broadcasted_iota(jnp.int32, (coarse_size, total_rows), 1)
    col_core = jnp.where(col >= nz * GROUP, 1, 0)
    rest = col - nz * GROUP * col_core
    wanted = modes * (CORES * (rest >> 3) + col_core) + (rest & 7)
    place = jnp.where((wanted == entry) & ((rest & 7) < modes), 1.0, 0.0)
    coarse[...] = exact(exact(pick, coarse_ref[...]), place)

    def invert(t, carry):
        where = t * LANES + lax.broadcasted_iota(jnp.int32, (LANES, LANES), 0)
        found = jnp.zeros((LANES, LANES), F32)
        for u in range(chunks):
            here = (u * LANES + lax.broadcasted_iota(jnp.int32, (LANES, LANES), 1)).astype(F32)
            line = jnp.broadcast_to(index_ref[:, u * LANES : (u + 1) * LANES], (LANES, LANES))
            found = jnp.where(line == where, here, found)
        line = jnp.sum(found.T, axis=0, keepdims=True).astype(jnp.int32)
        inverse[:, pl.ds(pl.multiple_of(t * LANES, LANES), LANES)] = jnp.broadcast_to(
            line, (GROUP, LANES)
        )
        return carry

    lax.fori_loop(0, chunks, invert, 0)

    greetings = len(peers) + has_prev.astype(jnp.int32) + has_next.astype(jnp.int32)
    pl.semaphore_wait(barrier, greetings)

    def faces(src, dst, ss, rs):
        up = copy(src.at[:, pl.ds(face, face)], dst.at[0], ss.at[0], rs.at[0], nxt)
        down = copy(src.at[:, pl.ds(0, face)], dst.at[1], ss.at[1], rs.at[1], prev)
        return up, down

    def start_faces(src, dst, ss, rs):
        up, down = faces(src, dst, ss, rs)

        @pl.when(has_next)
        def _():
            up.start()

        @pl.when(has_prev)
        def _():
            down.start()

    def wait_faces(src, dst, ss, rs):
        up, down = faces(src, dst, ss, rs)

        @pl.when(has_prev)
        def _():
            up.wait_recv()

        @pl.when(has_next)
        def _():
            down.wait_recv()

    def drain_faces(src, dst, ss, rs):
        up, down = faces(src, dst, ss, rs)

        @pl.when(has_next)
        def _():
            up.wait_send()

        @pl.when(has_prev)
        def _():
            down.wait_send()

    def halo_args(k):
        src = load_ref if k == 0 else sent.at[k - 1]
        return src, halo.at[k], halo_s.at[k], halo_r.at[k]

    basis_args = (own_basis, nbr_basis, basis_s, basis_r)
    start_faces(*basis_args)
    wait_faces(*basis_args)
    low, high = nbr_basis[0], nbr_basis[1]
    at_first, at_last = first_m.astype(F32), last_m.astype(F32)
    span_f[...] = jnp.zeros_like(span_f)
    span_f[0:GROUP, 0:face] = low * at_first
    span_f[GROUP : 2 * GROUP, 0:face] = own_basis[:, 0:face] + low * (1.0 - at_first)
    span_f[GROUP : 2 * GROUP, face:slots] = own_basis[:, face:slots] + high * (1.0 - at_last)
    span_f[2 * GROUP : 3 * GROUP, face:slots] = high * at_last
    s_high, s_low = split(span_f[...])
    span_h[...] = s_high
    span_l[...] = s_low

    def restrict(v):
        v_high, v_low = split(v)
        both = nt(jnp.concatenate([span_h[...], span_l[...]], axis=0), v_high)
        return both[:SPAN] + both[SPAN:] + nt(span_h[...], v_low)

    def expand(amounts):
        turned = amounts.T
        a_high, a_low = split(turned)
        both = mm(jnp.concatenate([a_high, a_low], axis=0), span_h[...])
        return both[:loads] + both[loads:] + mm(a_high, span_l[...])

    def put_restricted(k, v):
        terms = restrict(v)
        ybuf[k, y, 0:GROUP, 0:loads] = terms[GROUP : 2 * GROUP]
        ybuf[k, y, GROUP : 2 * GROUP, :] = jnp.concatenate(
            [terms[0:GROUP], terms[2 * GROUP : 3 * GROUP]], axis=1
        )

    def reduce(k, rows, between):
        own = ybuf.at[k, y, 0:rows]
        for peer in y_peers:
            copy(own, own, y_s.at[k], y_r.at[k], peer).start()
        take(ybuf.at[k, 0 : ny - 1, 0:rows], y_r.at[k])
        total = ybuf[k, 0, 0:rows]
        for i in range(1, ny):
            total = total + ybuf[k, i, 0:rows]
        xbuf[k, x, 0:rows] = total
        own = xbuf.at[k, x, 0:rows]
        for peer in x_peers:
            copy(own, own, x_s.at[k], x_r.at[k], peer).start()
        between()
        take(xbuf.at[k, 0 : nx - 1, 0:rows], x_r.at[k])
        total = xbuf[k, 0, 0:rows]
        for i in range(1, nx):
            total = total + xbuf[k, i, 0:rows]
        zbuf[k, core, z + 1, 0:rows] = total
        own = zbuf.at[k, core, z + 1, 0:rows]
        for peer in z_peers:
            copy(own, own, z_s.at[k], z_r.at[k], peer).start()
        take(zbuf.at[k, 0, 1:nz, 0:rows], z_r.at[k])
        mine = zbuf.at[k, core, 1 : nz + 1, 0:rows]
        swap = copy(mine, mine, c_s.at[k], c_r.at[k], partner)
        swap.start()
        swap.wait_recv()

    def drain(k, rows):
        take(ybuf.at[k, 0 : ny - 1, 0:rows], y_s.at[k])
        take(xbuf.at[k, 0 : nx - 1, 0:rows], x_s.at[k])
        take(zbuf.at[k, 0, 1:nz, 0:rows], z_s.at[k])
        take(zbuf.at[k, 0, 1 : nz + 1, 0:rows], c_s.at[k])

    def amounts(k):
        def part(core_id, shift, rows, lanes):
            return zbuf[k, core_id, 1 + shift : 1 + shift + nz, rows : rows + GROUP, lanes : lanes + loads]

        even = part(0, 0, 0, 0) + part(1, 0, GROUP, 0) + part(1, -1, GROUP, LANES - loads)
        odd = part(1, 0, 0, 0) + part(0, 1, GROUP, 0) + part(0, 0, GROUP, LANES - loads)
        half = nz * GROUP
        totals = jnp.concatenate([even.reshape(half, loads), odd.reshape(half, loads)], axis=0)
        return exact(coarse[...], totals)

    def scalar_sum(k, line):
        total = zbuf[k, 0, 1, line : line + 1, 0:loads]
        for core_id in range(CORES):
            for i in range(nz):
                if core_id or i:
                    total = total + zbuf[k, core_id, 1 + i, line : line + 1, 0:loads]
        return total

    def row_sum(v):
        part = v[:, 0:LANES]
        for t in range(1, chunks):
            part = part + v[:, t * LANES : (t + 1) * LANES]
        return jnp.sum(part.T, axis=0, keepdims=True)

    def spread(line):
        column = jnp.broadcast_to(line, (LANES, loads)).T
        return jnp.concatenate([column] * chunks, axis=1)

    low_weight = jnp.where(has_prev, 0.5, 1.0).astype(F32)
    high_weight = jnp.where(has_next, 0.5, 1.0).astype(F32)

    def weighted(v):
        return jnp.concatenate([v[:, 0:face] * low_weight, v[:, face:slots] * high_weight], axis=1)

    def assembled(k, v):
        return jnp.concatenate([v[:, 0:face] + halo[k, 0], v[:, face:slots] + halo[k, 1]], axis=1)

    def precondition(w, out):
        scaled = weighted(w).astype(BF16)
        for n in range(nblock):
            cols = slice(n * block, (n + 1) * block)
            weight = low_weight if n < nblock // 2 else high_weight
            out[:, cols] = weight * mm(scaled[:, cols], blocks_ref[n])

    def permute(src, order, dst, scale=None):
        for t in range(chunks):
            cols = slice(t * LANES, (t + 1) * LANES)
            line = jnp.broadcast_to(order[0:1, cols], (loads, LANES))
            lane, chunk = line & (LANES - 1), line >> 7
            found = jnp.zeros((loads, LANES), F32)
            for u in range(chunks):
                seen = jnp.take_along_axis(
                    src[:, u * LANES : (u + 1) * LANES], lane, axis=1, mode="promise_in_bounds"
                )
                found = jnp.where(chunk == u, seen, found)
            dst[:, cols] = found if scale is None else found * scale

    softness = 1.0 / jnp.broadcast_to(stiff_ref[...], (loads, LANES))

    def nothing():
        pass

    def starter(k):
        return functools.partial(start_faces, *halo_args(k))

    put_restricted(0, load_ref[...])
    reduce(0, 2 * GROUP, starter(0))
    wait_faces(*halo_args(0))
    resid[...] = assembled(0, load_ref[...])
    amount_r = amounts(0)
    proj[...] = resid[...] - expand(amount_r)

    precondition(proj[...], sent.at[0])
    put_restricted(1, sent[0])
    reduce(1, 2 * GROUP, starter(1))
    wait_faces(*halo_args(1))
    search0[...] = assembled(1, sent[0]) - expand(amounts(1))

    permute(search0, inverse, temp)
    oper_copy.wait()
    temp[...] = mm(temp[...].astype(BF16), oper[...])
    permute(temp, index_ref, sent.at[1], softness)
    put_restricted(2, sent[1])
    ybuf[2, y, 6:7, 0:loads] = row_sum(weighted(proj[...]) * search0[...])
    ybuf[2, y, 7:8, 0:loads] = row_sum(search0[...] * sent[1])
    reduce(2, 2 * GROUP, starter(2))
    rho0, gamma0 = scalar_sum(2, 6), scalar_sum(2, 7)
    step0 = rho0 / gamma0
    amount_r = amount_r - step0 * amounts(2)
    wait_faces(*halo_args(2))
    image_q[...] = assembled(2, sent[1])
    resid[...] = resid[...] - spread(step0) * image_q[...]
    proj[...] = resid[...] - expand(amount_r)

    precondition(proj[...], sent.at[2])
    put_restricted(3, sent[2])
    reduce(3, 2 * GROUP, starter(3))
    wait_faces(*halo_args(3))
    search1[...] = assembled(3, sent[2]) - expand(amounts(3))

    permute(search1, inverse, temp)
    t_high, t_low = split(temp[...])
    both = mm(jnp.concatenate([t_high, t_low], axis=0), oper[...])
    temp[...] = both[:loads] + both[loads:]
    permute(temp, index_ref, sent.at[3], softness)
    ybuf[4, y, 0:1, 0:loads] = row_sum(weighted(proj[...]) * search1[...])
    ybuf[4, y, 1:2, 0:loads] = row_sum(search1[...] * sent[3])
    ybuf[4, y, 2:3, 0:loads] = row_sum(search1[...] * sent[1])
    reduce(4, GROUP, starter(4))
    rho1 = scalar_sum(4, 0)
    beta = rho1 / rho0
    gamma1 = scalar_sum(4, 1) + 2.0 * beta * scalar_sum(4, 2) + beta * beta * gamma0
    step1 = rho1 / gamma1
    wait_faces(*halo_args(4))
    beta_all, step1_all = spread(beta), spread(step1)
    direction = search1[...] + beta_all * search0[...]
    mult_out[...] = spread(step0) * search0[...] + step1_all * direction
    resid_out[...] = resid[...] - step1_all * (assembled(4, sent[3]) + beta_all * image_q[...])

    drain_faces(*basis_args)
    for k in range(HALOS):
        drain_faces(*halo_args(k))
    for k in range(SUMS):
        drain(k, 2 * GROUP if k < SUMS - 1 else GROUP)


def per_device(
    dual_load, dual_operator, index_map, stiffness, coarse_basis, dirichlet_blocks, coarse_inverse
):
    loads, face = dual_load.shape[2], dual_load.shape[4]
    slots = 2 * face
    modes = coarse_basis.shape[2]
    clusters, members = lax.axis_size("cluster"), lax.axis_size("member")
    nz, ny, nx = clusters // CORES, NY, members // NY
    vmem = pl.BlockSpec(memory_space=pltpu.VMEM)
    vector = pltpu.VMEM((loads, slots), F32)
    dma = pltpu.SemaphoreType.DMA
    mult, resid = pl.pallas_call(
        kernel,
        out_shape=[jax.ShapeDtypeStruct((loads, slots), F32)] * 2,
        in_specs=[vmem] * 6 + [pl.BlockSpec(memory_space=pl.ANY)],
        out_specs=[vmem] * 2,
        scratch_shapes=[
            pltpu.VMEM((slots, slots), BF16),
            pltpu.VMEM((GROUP, slots), F32),
            pltpu.VMEM((2, GROUP, face), F32),
            pltpu.VMEM((SPAN, slots), F32),
            pltpu.VMEM((SPAN, slots), BF16),
            pltpu.VMEM((SPAN, slots), BF16),
            pltpu.VMEM((SPAN, clusters * GROUP), F32),
            pltpu.VMEM((GROUP, slots), jnp.int32),
            pltpu.VMEM((HALOS, 2, loads, face), F32),
            pltpu.VMEM((HALOS - 1, loads, slots), F32),
            vector,
            vector,
            vector,
            vector,
            vector,
            vector,
            pltpu.VMEM((SUMS, ny, 2 * GROUP, LANES), F32),
            pltpu.VMEM((SUMS, nx, 2 * GROUP, LANES), F32),
            pltpu.VMEM((SUMS, CORES, nz + 2, 2 * GROUP, LANES), F32),
            dma,
            dma((2,)),
            dma((2,)),
            dma((HALOS, 2)),
            dma((HALOS, 2)),
        ]
        + [dma((SUMS,))] * 8,
        compiler_params=pltpu.CompilerParams(
            collective_id=0, has_side_effects=True, vmem_limit_bytes=56 * 2**20
        ),
        name="pcpg",
    )(
        dual_load.reshape(loads, slots),
        coarse_basis.reshape(modes, 1, slots),
        dirichlet_blocks.reshape(dirichlet_blocks.shape[2:]),
        coarse_inverse,
        index_map.reshape(1, slots),
        stiffness,
        dual_operator,
    )
    return mult.reshape(dual_load.shape), resid.reshape(dual_load.shape)


def solution(mesh):
    five = P("cluster", "member", None, None, None)
    in_specs = (
        five,
        P(),
        P("cluster", "member", None),
        P("cluster", "member"),
        P("cluster", "member", None, None),
        five,
        P(),
    )
    return jax.shard_map(
        per_device, mesh=mesh, in_specs=in_specs, out_specs=(five, five), check_vma=False
    )
```

```python
import jax
import jax.numpy as jnp
from jax import lax
from jax.experimental import pallas as pl
from jax.experimental.pallas import tpu as pltpu
from jax.sharding import PartitionSpec as P

MESH = pl.DeviceIdType.MESH
NY = 8
CORES = 2
GROUP = 8
SPAN = 32
LANES = 128
HALOS = 5
SUMS = 3
WIDE = 3 * GROUP
F32 = jnp.float32
BF16 = jnp.bfloat16


def nt(a, b):
    return lax.dot_general(a, b, (((1,), (1,)), ((), ())), preferred_element_type=F32)


def mm(a, b):
    return jnp.dot(a, b, preferred_element_type=F32)


def exact(a, b):
    return jnp.dot(a, b, precision=lax.Precision.HIGHEST, preferred_element_type=F32)


def split(v):
    high = v.astype(BF16)
    return high, (v - high.astype(F32)).astype(BF16)


def kernel(
    basis_ref,
    coarse_ref,
    index_ref,
    stiff_ref,
    load_hbm,
    blocks_hbm,
    oper_hbm,
    mult_out,
    resid_out,
    raw,
    blocks,
    oper,
    load,
    own_basis,
    nbr_basis,
    span_f,
    span_h,
    span_l,
    order_h,
    order_l,
    wide,
    coarse,
    amount,
    gram,
    inverse,
    halo,
    halo_span,
    sent,
    sent_span,
    resid,
    proj,
    search0,
    search1,
    image_q,
    turned0,
    turned1,
    image0,
    image1,
    ybuf,
    xbuf,
    zbuf,
    local_sem,
    basis_s,
    basis_r,
    span_s,
    span_r,
    halo_s,
    halo_r,
    y_s,
    y_r,
    x_s,
    x_r,
    z_s,
    z_r,
    c_s,
    c_r,
):
    loads, slots = load.shape
    face = slots // 2
    chunks = slots // LANES
    modes = basis_ref.shape[0]
    nblock, block = blocks.shape[:2]
    nz = zbuf.shape[1] - 2
    nx = xbuf.shape[1]
    ny = ybuf.shape[1]
    members = nx * ny
    clusters = nz * CORES
    c = lax.axis_index("cluster")
    m = lax.axis_index("member")
    z, core = c // CORES, lax.rem(c, CORES)
    x, y = m // ny, lax.rem(m, ny)
    chain = c * members + m
    last = clusters * members - 1
    has_prev, has_next = chain > 0, chain < last
    first_m, last_m = m == 0, m == members - 1
    prev = (jnp.where(first_m, c - 1, c), jnp.where(first_m, members - 1, m - 1))
    nxt = (jnp.where(last_m, c + 1, c), jnp.where(last_m, 0, m + 1))
    y_peers = [(c, x * ny + lax.rem(y + i, ny)) for i in range(1, ny)]
    x_peers = [(c, lax.rem(x + i, nx) * ny + y) for i in range(1, nx)]
    z_peers = [(lax.rem(z + i, nz) * CORES + core, m) for i in range(1, nz)]
    partner = (z * CORES + 1 - core, m)

    def copy(src, dst, ss, rs, device):
        return pltpu.make_async_remote_copy(
            src_ref=src, dst_ref=dst, send_sem=ss, recv_sem=rs, device_id=device, device_id_type=MESH
        )

    def take(ref, sem):
        pltpu.make_async_copy(ref, ref, sem).wait()

    barrier = pltpu.get_barrier_semaphore()
    peers = z_peers + y_peers + x_peers + [partner]
    for peer in peers:
        pl.semaphore_signal(barrier, inc=1, device_id=peer, device_id_type=MESH)

    @pl.when(has_prev)
    def _():
        pl.semaphore_signal(barrier, inc=1, device_id=prev, device_id_type=MESH)

    @pl.when(has_next)
    def _():
        pl.semaphore_signal(barrier, inc=1, device_id=nxt, device_id_type=MESH)

    raw_copy = pltpu.make_async_copy(load_hbm, raw, local_sem.at[0])
    blocks_copy = pltpu.make_async_copy(blocks_hbm, blocks, local_sem.at[1])
    oper_copy = pltpu.make_async_copy(oper_hbm, oper, local_sem.at[2])
    raw_copy.start()
    blocks_copy.start()
    oper_copy.start()

    own_basis[...] = jnp.zeros_like(own_basis)
    for k in range(modes):
        own_basis[k : k + 1, :] = basis_ref[k]
    zero_tile = jnp.zeros((WIDE, LANES), F32)
    for k in range(SUMS):
        ybuf[k, y] = zero_tile
        for core_id in range(CORES):
            zbuf[k, 0, core_id] = zero_tile
            zbuf[k, nz + 1, core_id] = zero_tile
    amount[...] = jnp.zeros_like(amount)

    @pl.when(jnp.logical_not(has_prev))
    def _():
        nbr_basis[0] = jnp.zeros((GROUP, face), F32)
        halo_span[0] = jnp.zeros((SPAN, face), F32)
        for k in range(HALOS):
            halo[k, 0] = jnp.zeros((loads, face), F32)

    @pl.when(jnp.logical_not(has_next))
    def _():
        nbr_basis[1] = jnp.zeros((GROUP, face), F32)
        halo_span[1] = jnp.zeros((SPAN, face), F32)
        for k in range(HALOS):
            halo[k, 1] = jnp.zeros((loads, face), F32)

    raw_copy.wait()
    for f in range(2):
        for t in range(chunks // 2):
            start = f * face + t * LANES
            load[:, start : start + LANES] = raw[pl.ds(2 * t + f, loads, stride=chunks), :]

    coarse_size = coarse_ref.shape[0]
    total_rows = clusters * GROUP

    def placed(row, entry):
        return jnp.where((modes * (row >> 3) + (row & 7) == entry) & ((row & 7) < modes), 1.0, 0.0)

    shape = (total_rows, coarse_size)
    down = placed(lax.broadcasted_iota(jnp.int32, shape, 0), lax.broadcasted_iota(jnp.int32, shape, 1))
    shape = (coarse_size, total_rows)
    across = placed(
        lax.broadcasted_iota(jnp.int32, shape, 1), lax.broadcasted_iota(jnp.int32, shape, 0)
    )
    coarse[...] = exact(exact(down, coarse_ref[...]), across)

    def invert(t, carry):
        where = t * LANES + lax.broadcasted_iota(jnp.int32, (LANES, LANES), 0)
        found = jnp.zeros((LANES, LANES), F32)
        for u in range(chunks):
            here = (u * LANES + lax.broadcasted_iota(jnp.int32, (LANES, LANES), 1)).astype(F32)
            line = jnp.broadcast_to(index_ref[:, u * LANES : (u + 1) * LANES], (LANES, LANES))
            found = jnp.where(line == where, here, found)
        line = jnp.sum(found.T, axis=0, keepdims=True).astype(jnp.int32)
        inverse[:, pl.ds(pl.multiple_of(t * LANES, LANES), LANES)] = jnp.broadcast_to(
            line, (GROUP, LANES)
        )
        return carry

    lax.fori_loop(0, chunks, invert, 0)
    blocks_copy.wait()

    greetings = len(peers) + has_prev.astype(jnp.int32) + has_next.astype(jnp.int32)
    pl.semaphore_wait(barrier, greetings)

    def faces(src, dst, ss, rs):
        up = copy(src.at[:, pl.ds(face, face)], dst.at[0], ss.at[0], rs.at[0], nxt)
        down = copy(src.at[:, pl.ds(0, face)], dst.at[1], ss.at[1], rs.at[1], prev)
        return up, down

    def start_faces(args):
        up, down = faces(*args)

        @pl.when(has_next)
        def _():
            up.start()

        @pl.when(has_prev)
        def _():
            down.start()

    def wait_faces(args):
        up, down = faces(*args)

        @pl.when(has_prev)
        def _():
            up.wait_recv()

        @pl.when(has_next)
        def _():
            down.wait_recv()

    def drain_faces(args):
        up, down = faces(*args)

        @pl.when(has_next)
        def _():
            up.wait_send()

        @pl.when(has_prev)
        def _():
            down.wait_send()

    basis_args = (own_basis, nbr_basis, basis_s, basis_r)
    span_args = (sent_span, halo_span, span_s, span_r)
    halo_args = [
        (load if k == 0 else sent.at[k - 1], halo.at[k], halo_s.at[k], halo_r.at[k])
        for k in range(HALOS)
    ]

    def reduce(k, rows, after_y, after_x, after_z):
        own = ybuf.at[k, y, 0:rows]
        for peer in y_peers:
            copy(own, own, y_s.at[k], y_r.at[k], peer).start()
        after_y()
        take(ybuf.at[k, 0 : ny - 1, 0:rows], y_r.at[k])
        total = ybuf[k, 0, 0:rows]
        for i in range(1, ny):
            total = total + ybuf[k, i, 0:rows]
        xbuf[k, x, 0:rows] = total
        own = xbuf.at[k, x, 0:rows]
        for peer in x_peers:
            copy(own, own, x_s.at[k], x_r.at[k], peer).start()
        after_x()
        take(xbuf.at[k, 0 : nx - 1, 0:rows], x_r.at[k])
        total = xbuf[k, 0, 0:rows]
        for i in range(1, nx):
            total = total + xbuf[k, i, 0:rows]
        zbuf[k, z + 1, core, 0:rows] = total
        own = zbuf.at[k, z + 1, core, 0:rows]
        for peer in z_peers:
            copy(own, own, z_s.at[k], z_r.at[k], peer).start()
        after_z()
        take(zbuf.at[k, 1:nz, 0, 0:rows], z_r.at[k])
        mine = zbuf.at[k, 1 : nz + 1, core, 0:rows]
        swap = copy(mine, mine, c_s.at[k], c_r.at[k], partner)
        swap.start()
        swap.wait_recv()

    def drain(k, rows):
        take(ybuf.at[k, 0 : ny - 1, 0:rows], y_s.at[k])
        take(xbuf.at[k, 0 : nx - 1, 0:rows], x_s.at[k])
        take(zbuf.at[k, 1:nz, 0, 0:rows], z_s.at[k])
        take(zbuf.at[k, 1 : nz + 1, 0, 0:rows], c_s.at[k])

    def gathered(k):
        return zbuf[k].reshape(CORES * (nz + 2), WIDE, LANES)

    def fold(parts):
        total = (
            parts[2 : 2 + clusters, GROUP : 2 * GROUP]
            + parts[3 : 3 + clusters, 0:GROUP]
            + parts[1 : 1 + clusters, 2 * GROUP : WIDE]
        )
        return total.reshape(total_rows, LANES)

    def solve(totals):
        amounts = exact(coarse[...], totals)
        amount[GROUP : GROUP + total_rows, 0:loads] = amounts
        return amount[pl.ds(pl.multiple_of(GROUP * c, GROUP), SPAN), 0:loads]

    def gram_amount():
        parts = [
            exact(gram[j], amount[GROUP * j : GROUP * j + SPAN, 0:loads]) for j in range(clusters)
        ]
        rows = []
        for j in range(clusters):
            line = parts[j][GROUP : 2 * GROUP]
            if j + 1 < clusters:
                line = line + parts[j + 1][0:GROUP]
            if j > 0:
                line = line + parts[j - 1][2 * GROUP : WIDE]
            rows.append(line)
        return jnp.concatenate(rows, axis=0)

    def restrict(high, low, v):
        rows = high.shape[0]
        v_high, v_low = split(v)
        both = nt(jnp.concatenate([high, low], axis=0), v_high)
        return both[:rows] + both[rows:] + nt(high, v_low)

    def expand(amounts, rows):
        a_high, a_low = split(amounts.T)
        both = mm(jnp.concatenate([a_high, a_low], axis=0), span_h[0:rows])
        return both[:loads] + both[loads:] + mm(a_high, span_l[0:rows])

    def row_sum(v):
        part = v[:, 0:LANES]
        for t in range(1, chunks):
            part = part + v[:, t * LANES : (t + 1) * LANES]
        return jnp.sum(part.T, axis=0, keepdims=True)

    def spread(line):
        column = jnp.broadcast_to(line, (LANES, loads)).T
        return jnp.concatenate([column] * chunks, axis=1)

    low_weight = jnp.where(has_prev, 0.5, 1.0).astype(F32)
    high_weight = jnp.where(has_next, 0.5, 1.0).astype(F32)

    def weighted(v):
        return jnp.concatenate([v[:, 0:face] * low_weight, v[:, face:slots] * high_weight], axis=1)

    def assembled(k, v):
        return jnp.concatenate([v[:, 0:face] + halo[k, 0], v[:, face:slots] + halo[k, 1]], axis=1)

    def precondition(v, out, parts=2):
        rows = v.shape[0]
        pair = jnp.concatenate(split(v)[:parts], axis=0)
        for n in range(nblock):
            cols = slice(n * block, (n + 1) * block)
            weight = low_weight if n < nblock // 2 else high_weight
            both = mm(pair[:, cols], blocks[n])
            if parts == 2:
                both = both[:rows] + both[rows:]
            out[:, cols] = (weight * weight) * both

    def permute(src, order, dst):
        rows = src.shape[0]
        for t in range(chunks):
            cols = slice(t * LANES, (t + 1) * LANES)
            line = jnp.broadcast_to(order[0:1, cols], (rows, LANES))
            lane, chunk = line & (LANES - 1), line >> 7
            found = jnp.zeros((rows, LANES), F32)
            for u in range(chunks):
                seen = jnp.take_along_axis(
                    src[:, u * LANES : (u + 1) * LANES], lane, axis=1, mode="promise_in_bounds"
                )
                found = jnp.where(chunk == u, seen, found)
            dst[:, cols] = found

    softness = 1.0 / jnp.broadcast_to(stiff_ref[...], (loads, LANES))
    softness = jnp.concatenate([softness] * chunks, axis=1)

    def nothing():
        pass

    start_faces(basis_args)
    start_faces(halo_args[0])
    wait_faces(basis_args)
    low, high = nbr_basis[0], nbr_basis[1]
    at_first, at_last = first_m.astype(F32), last_m.astype(F32)
    span_f[...] = jnp.zeros_like(span_f)
    span_f[0:GROUP, 0:face] = low * at_first
    span_f[GROUP : 2 * GROUP, 0:face] = own_basis[:, 0:face] + low * (1.0 - at_first)
    span_f[GROUP : 2 * GROUP, face:slots] = own_basis[:, face:slots] + high * (1.0 - at_last)
    span_f[2 * GROUP : WIDE, face:slots] = high * at_last
    s_high, s_low = split(span_f[...])
    span_h[0:SPAN] = s_high
    span_l[0:SPAN] = s_low
    precondition(span_f[...], sent_span)
    own_gram = restrict(span_h[0:SPAN], span_l[0:SPAN], sent_span[...])
    permute(span_f, inverse, wide)
    s_high, s_low = split(wide[...])
    order_h[0:SPAN] = s_high
    order_l[0:SPAN] = s_low

    wait_faces(halo_args[0])
    resid[...] = assembled(0, load[...])
    precondition(resid[...], sent.at[0])

    terms = restrict(span_h[0:SPAN], span_l[0:SPAN], sent[0])
    o_high, o_low = split(jnp.concatenate([own_basis[...], jnp.zeros_like(own_basis)], axis=0))
    own_terms = restrict(o_high, o_low, resid[...])
    ybuf[0, y, 0:GROUP, :] = jnp.concatenate(
        [terms[0:GROUP], own_gram[0:GROUP], own_gram[GROUP : 2 * GROUP]], axis=1
    )
    ybuf[0, y, GROUP : 2 * GROUP, :] = jnp.concatenate(
        [terms[GROUP : 2 * GROUP], own_terms[0:GROUP]], axis=1
    )
    ybuf[0, y, 2 * GROUP : WIDE, 0:loads] = terms[2 * GROUP : WIDE]
    ybuf[0, y, 2 * GROUP : WIDE, loads : loads + SPAN] = own_gram[2 * GROUP : WIDE]

    def assemble_span():
        wait_faces(span_args)
        low, high = halo_span[0], halo_span[1]
        none = jnp.zeros((GROUP, face), F32)
        low_moved = jnp.concatenate([low[GROUP:SPAN], none], axis=0)
        high_moved = jnp.concatenate([none, high[0 : SPAN - GROUP]], axis=0)
        low = jnp.where(first_m, low_moved, low)
        high = jnp.where(last_m, high_moved, high)
        wide[:, 0:face] = sent_span[:, 0:face] + low
        wide[:, face:slots] = sent_span[:, face:slots] + high
        t_high, t_low = split(wide[...])
        span_h[SPAN : 2 * SPAN] = t_high
        span_l[SPAN : 2 * SPAN] = t_low
        permute(wide, inverse, span_f)
        t_high, t_low = split(span_f[...])
        order_h[SPAN : 2 * SPAN] = t_high
        order_l[SPAN : 2 * SPAN] = t_low

    def start_first():
        start_faces(span_args)
        start_faces(halo_args[1])

    reduce(0, WIDE, nothing, start_first, assemble_span)
    parts = gathered(0)
    for j in range(clusters):
        gram[j] = jnp.concatenate(
            [
                parts[j + 2, 0:GROUP, loads : loads + SPAN],
                parts[j + 2, 0:GROUP, loads + SPAN : LANES],
                parts[j + 2, 2 * GROUP : WIDE, loads : loads + SPAN],
            ],
            axis=0,
        )
    totals = parts[2 : 2 + clusters, GROUP : 2 * GROUP, LANES - loads : LANES]
    amount_r = solve(totals.reshape(total_rows, loads))
    reduced = fold(parts)[:, 0:loads] - gram_amount()
    amount_y = solve(reduced)
    wait_faces(halo_args[1])
    search0[...] = assembled(1, sent[0]) - expand(
        jnp.concatenate([amount_y, amount_r], axis=0), 2 * SPAN
    )
    proj[...] = resid[...] - expand(amount_r, SPAN)

    permute(search0, inverse, turned0)
    oper_copy.wait()
    image0[...] = softness * mm(turned0[...].astype(BF16), oper[...])
    terms = restrict(order_h[...], order_l[...], image0[...])
    ybuf[1, y] = jnp.concatenate([terms[0:WIDE], terms[SPAN : SPAN + WIDE]], axis=1)
    ybuf[1, y, 2 * GROUP - 2 : 2 * GROUP - 1, 0:loads] = row_sum(weighted(proj[...]) * search0[...])
    ybuf[1, y, 2 * GROUP - 1 : 2 * GROUP, 0:loads] = row_sum(turned0[...] * image0[...])
    reduce(
        1,
        WIDE,
        lambda: permute(image0, index_ref, sent.at[1]),
        lambda: start_faces(halo_args[2]),
        nothing,
    )
    parts = gathered(1)
    sums = jnp.sum(parts[2 : 2 + clusters, GROUP : 2 * GROUP, 0:loads], axis=0)
    rho0, gamma0 = sums[GROUP - 2 : GROUP - 1], sums[GROUP - 1 : GROUP]
    step0 = rho0 / gamma0
    totals = fold(parts)
    amount_r = amount_r - step0 * solve(totals[:, 0:loads])
    reduced = reduced - step0 * (totals[:, LANES - loads : LANES] - gram_amount())
    wait_faces(halo_args[2])
    image_q[...] = assembled(2, sent[1])
    resid[...] = resid[...] - spread(step0) * image_q[...]
    proj[...] = resid[...] - expand(amount_r, SPAN)
    precondition(proj[...], sent.at[2], 1)
    start_faces(halo_args[3])
    amount_y = solve(reduced)
    spread_y = expand(amount_y, SPAN)
    wait_faces(halo_args[3])
    search1[...] = assembled(3, sent[2]) - spread_y

    permute(search1, inverse, turned1)
    t_high, t_low = split(turned1[...])
    both = mm(jnp.concatenate([t_high, t_low], axis=0), oper[...])
    image1[...] = softness * (both[:loads] + both[loads:])
    ybuf[2, y, 0:1, 0:loads] = row_sum(weighted(proj[...]) * search1[...])
    ybuf[2, y, 1:2, 0:loads] = row_sum(turned1[...] * image1[...])
    ybuf[2, y, 2:3, 0:loads] = row_sum(turned1[...] * image0[...])
    reduce(
        2,
        GROUP,
        lambda: permute(image1, index_ref, sent.at[3]),
        lambda: start_faces(halo_args[4]),
        nothing,
    )
    sums = zbuf[2, 1, 0, 0:GROUP, 0:loads]
    for j in range(1, clusters):
        sums = sums + zbuf[2, 1 + j // CORES, j % CORES, 0:GROUP, 0:loads]
    rho1 = sums[0:1]
    beta = rho1 / rho0
    gamma1 = sums[1:2] + 2.0 * beta * sums[2:3] + beta * beta * gamma0
    step1 = rho1 / gamma1
    wait_faces(halo_args[4])
    beta_all, step0_all, step1_all = (spread(v)[:, 0:LANES] for v in (beta, step0, step1))
    for f in range(2):
        for t in range(chunks // 2):
            cols = slice(f * face + t * LANES, f * face + (t + 1) * LANES)
            near = slice(t * LANES, (t + 1) * LANES)
            rows = pl.ds(2 * t + f, loads, stride=chunks)
            first = search0[:, cols]
            direction = search1[:, cols] + beta_all * first
            mult_out[rows, :] = step0_all * first + step1_all * direction
            image = sent[3, :, cols] + halo[4, f, :, near] + beta_all * image_q[:, cols]
            resid_out[rows, :] = resid[:, cols] - step1_all * image

    drain_faces(basis_args)
    drain_faces(span_args)
    for k in range(HALOS):
        drain_faces(halo_args[k])
    for k in range(SUMS):
        drain(k, WIDE if k < SUMS - 1 else GROUP)


def per_device(
    dual_load, dual_operator, index_map, stiffness, coarse_basis, dirichlet_blocks, coarse_inverse
):
    loads, face = dual_load.shape[2], dual_load.shape[4]
    slots = 2 * face
    modes = coarse_basis.shape[2]
    clusters, members = lax.axis_size("cluster"), lax.axis_size("member")
    nz, ny, nx = clusters // CORES, NY, members // NY
    blocks_shape = dirichlet_blocks.shape[2:]
    vmem = pl.BlockSpec(memory_space=pltpu.VMEM)
    in_place = pl.BlockSpec(memory_space=pl.ANY)
    vector = pltpu.VMEM((loads, slots), F32)
    span = pltpu.VMEM((SPAN, slots), F32)
    spans = pltpu.VMEM((2 * SPAN, slots), BF16)
    dma = pltpu.SemaphoreType.DMA
    rows = loads * slots // LANES
    lines = (loads, face // LANES, 2, LANES)
    load = dual_load.reshape(loads, 2, face // LANES, LANES).transpose(0, 2, 1, 3)
    outs = pl.pallas_call(
        kernel,
        out_shape=[jax.ShapeDtypeStruct((rows, LANES), F32)] * 2,
        in_specs=[vmem] * 4 + [in_place] * 3,
        out_specs=[vmem] * 2,
        scratch_shapes=[
            pltpu.VMEM((rows, LANES), F32),
            pltpu.VMEM(blocks_shape, BF16),
            pltpu.VMEM((slots, slots), BF16),
            vector,
            pltpu.VMEM((GROUP, slots), F32),
            pltpu.VMEM((2, GROUP, face), F32),
            span,
            spans,
            spans,
            spans,
            spans,
            span,
            pltpu.VMEM((clusters * GROUP, clusters * GROUP), F32),
            pltpu.VMEM(((clusters + 3) * GROUP, LANES), F32),
            pltpu.VMEM((clusters, WIDE, SPAN), F32),
            pltpu.VMEM((GROUP, slots), jnp.int32),
            pltpu.VMEM((HALOS, 2, loads, face), F32),
            pltpu.VMEM((2, SPAN, face), F32),
            pltpu.VMEM((HALOS - 1, loads, slots), F32),
            span,
        ]
        + [vector] * 9
        + [
            pltpu.VMEM((SUMS, ny, WIDE, LANES), F32),
            pltpu.VMEM((SUMS, nx, WIDE, LANES), F32),
            pltpu.VMEM((SUMS, nz + 2, CORES, WIDE, LANES), F32),
            dma((3,)),
            dma((2,)),
            dma((2,)),
            dma((2,)),
            dma((2,)),
            dma((HALOS, 2)),
            dma((HALOS, 2)),
        ]
        + [dma((SUMS,))] * 8,
        compiler_params=pltpu.CompilerParams(
            collective_id=0, has_side_effects=True, vmem_limit_bytes=56 * 2**20
        ),
        name="pcpg",
    )(
        coarse_basis.reshape(modes, 1, slots),
        coarse_inverse,
        index_map.reshape(1, slots),
        stiffness,
        load.reshape(rows, LANES),
        dirichlet_blocks.reshape(blocks_shape),
        dual_operator,
    )
    mult, resid = (out.reshape(lines).transpose(0, 2, 1, 3).reshape(dual_load.shape) for out in outs)
    return mult, resid


def solution(mesh):
    five = P("cluster", "member", None, None, None)
    in_specs = (
        five,
        P(),
        P("cluster", "member", None),
        P("cluster", "member"),
        P("cluster", "member", None, None),
        five,
        P(),
    )
    return jax.shard_map(
        per_device, mesh=mesh, in_specs=in_specs, out_specs=(five, five), check_vma=False
    )
```

```python
import jax
import jax.numpy as jnp
from jax import lax
from jax.experimental import pallas as pl
from jax.experimental.pallas import tpu as pltpu
from jax.sharding import PartitionSpec as P

MESH = pl.DeviceIdType.MESH
NY = 8
CORES = 2
GROUP = 8
SPAN = 32
LANES = 128
HALOS = 5
SUMS = 3
WIDE = 3 * GROUP
F32 = jnp.float32
BF16 = jnp.bfloat16


def nt(a, b):
    return lax.dot_general(a, b, (((1,), (1,)), ((), ())), preferred_element_type=F32)


def mm(a, b):
    return jnp.dot(a, b, preferred_element_type=F32)


def exact(a, b):
    return jnp.dot(a, b, precision=lax.Precision.HIGHEST, preferred_element_type=F32)


def split(v):
    high = v.astype(BF16)
    return high, (v - high.astype(F32)).astype(BF16)


def kernel(
    basis_ref,
    coarse_ref,
    index_ref,
    stiff_ref,
    load_hbm,
    blocks_hbm,
    oper_hbm,
    mult_out,
    resid_out,
    raw,
    blocks,
    oper,
    load,
    own_basis,
    nbr_basis,
    span_f,
    span_h,
    span_l,
    order_h,
    order_l,
    wide,
    coarse,
    amount,
    gram,
    inverse,
    halo,
    halo_span,
    sent,
    sent_span,
    resid,
    proj,
    search0,
    search1,
    image_q,
    turned0,
    turned1,
    image0,
    image1,
    ybuf,
    xbuf,
    zbuf,
    local_sem,
    basis_s,
    basis_r,
    span_s,
    span_r,
    halo_s,
    halo_r,
    y_s,
    y_r,
    x_s,
    x_r,
    z_s,
    z_r,
    c_s,
    c_r,
):
    loads, slots = load.shape
    face = slots // 2
    chunks = slots // LANES
    modes = basis_ref.shape[0]
    nblock, block = blocks.shape[:2]
    nz = zbuf.shape[1] - 2
    nx = xbuf.shape[1]
    ny = ybuf.shape[1]
    members = nx * ny
    clusters = nz * CORES
    c = lax.axis_index("cluster")
    m = lax.axis_index("member")
    z, core = c // CORES, lax.rem(c, CORES)
    x, y = m // ny, lax.rem(m, ny)
    chain = c * members + m
    last = clusters * members - 1
    has_prev, has_next = chain > 0, chain < last
    first_m, last_m = m == 0, m == members - 1
    prev = (jnp.where(first_m, c - 1, c), jnp.where(first_m, members - 1, m - 1))
    nxt = (jnp.where(last_m, c + 1, c), jnp.where(last_m, 0, m + 1))
    y_peers = [(c, x * ny + lax.rem(y + i, ny)) for i in range(1, ny)]
    x_peers = [(c, lax.rem(x + i, nx) * ny + y) for i in range(1, nx)]
    z_peers = [(lax.rem(z + i, nz) * CORES + core, m) for i in range(1, nz)]
    partner = (z * CORES + 1 - core, m)

    def copy(src, dst, ss, rs, device):
        return pltpu.make_async_remote_copy(
            src_ref=src, dst_ref=dst, send_sem=ss, recv_sem=rs, device_id=device, device_id_type=MESH
        )

    def take(ref, sem):
        pltpu.make_async_copy(ref, ref, sem).wait()

    barrier = pltpu.get_barrier_semaphore()
    peers = z_peers + y_peers + x_peers + [partner]
    for peer in peers:
        pl.semaphore_signal(barrier, inc=1, device_id=peer, device_id_type=MESH)

    @pl.when(has_prev)
    def _():
        pl.semaphore_signal(barrier, inc=1, device_id=prev, device_id_type=MESH)

    @pl.when(has_next)
    def _():
        pl.semaphore_signal(barrier, inc=1, device_id=nxt, device_id_type=MESH)

    raw_copy = pltpu.make_async_copy(load_hbm, raw, local_sem.at[0])
    blocks_copy = pltpu.make_async_copy(blocks_hbm, blocks, local_sem.at[1])
    oper_copy = pltpu.make_async_copy(oper_hbm, oper, local_sem.at[2])
    raw_copy.start()
    blocks_copy.start()
    oper_copy.start()

    own_basis[...] = jnp.zeros_like(own_basis)
    for k in range(modes):
        own_basis[k : k + 1, :] = basis_ref[k]
    raw_copy.wait()
    for f in range(2):
        for t in range(chunks // 2):
            start = f * face + t * LANES
            load[:, start : start + LANES] = raw[pl.ds(2 * t + f, loads, stride=chunks), :]

    greetings = len(peers) + has_prev.astype(jnp.int32) + has_next.astype(jnp.int32)
    pl.semaphore_wait(barrier, greetings)

    def faces(src, dst, ss, rs):
        up = copy(src.at[:, pl.ds(face, face)], dst.at[0], ss.at[0], rs.at[0], nxt)
        down = copy(src.at[:, pl.ds(0, face)], dst.at[1], ss.at[1], rs.at[1], prev)
        return up, down

    def start_faces(args):
        up, down = faces(*args)

        @pl.when(has_next)
        def _():
            up.start()

        @pl.when(has_prev)
        def _():
            down.start()

    def wait_faces(args):
        up, down = faces(*args)

        @pl.when(has_prev)
        def _():
            up.wait_recv()

        @pl.when(has_next)
        def _():
            down.wait_recv()

    def drain_faces(args):
        up, down = faces(*args)

        @pl.when(has_next)
        def _():
            up.wait_send()

        @pl.when(has_prev)
        def _():
            down.wait_send()

    basis_args = (own_basis, nbr_basis, basis_s, basis_r)
    span_args = (sent_span, halo_span, span_s, span_r)
    halo_args = [
        (load if k == 0 else sent.at[k - 1], halo.at[k], halo_s.at[k], halo_r.at[k])
        for k in range(HALOS)
    ]

    def reduce(k, rows, after_y, after_x, after_z):
        own = ybuf.at[k, y, 0:rows]
        for peer in y_peers:
            copy(own, own, y_s.at[k], y_r.at[k], peer).start()
        after_y()
        take(ybuf.at[k, 0 : ny - 1, 0:rows], y_r.at[k])
        total = ybuf[k, 0, 0:rows]
        for i in range(1, ny):
            total = total + ybuf[k, i, 0:rows]
        xbuf[k, x, 0:rows] = total
        own = xbuf.at[k, x, 0:rows]
        for peer in x_peers:
            copy(own, own, x_s.at[k], x_r.at[k], peer).start()
        after_x()
        take(xbuf.at[k, 0 : nx - 1, 0:rows], x_r.at[k])
        total = xbuf[k, 0, 0:rows]
        for i in range(1, nx):
            total = total + xbuf[k, i, 0:rows]
        zbuf[k, z + 1, core, 0:rows] = total
        own = zbuf.at[k, z + 1, core, 0:rows]
        for peer in z_peers:
            copy(own, own, z_s.at[k], z_r.at[k], peer).start()
        after_z()
        take(zbuf.at[k, 1:nz, 0, 0:rows], z_r.at[k])
        mine = zbuf.at[k, 1 : nz + 1, core, 0:rows]
        swap = copy(mine, mine, c_s.at[k], c_r.at[k], partner)
        swap.start()
        swap.wait_recv()

    def drain(k, rows):
        take(ybuf.at[k, 0 : ny - 1, 0:rows], y_s.at[k])
        take(xbuf.at[k, 0 : nx - 1, 0:rows], x_s.at[k])
        take(zbuf.at[k, 1:nz, 0, 0:rows], z_s.at[k])
        take(zbuf.at[k, 1 : nz + 1, 0, 0:rows], c_s.at[k])

    def gathered(k):
        return zbuf[k].reshape(CORES * (nz + 2), WIDE, LANES)

    def fold(parts):
        total = (
            parts[2 : 2 + clusters, GROUP : 2 * GROUP]
            + parts[3 : 3 + clusters, 0:GROUP]
            + parts[1 : 1 + clusters, 2 * GROUP : WIDE]
        )
        return total.reshape(total_rows, LANES)

    def solve(totals):
        t_high, t_low = split(totals)
        both = mm(coarse[...], t_high)
        amounts = both[:total_rows] + both[total_rows:] + mm(coarse[0:total_rows], t_low)
        amount[GROUP : GROUP + total_rows, 0:loads] = amounts
        return amount[pl.ds(pl.multiple_of(GROUP * c, GROUP), SPAN), 0:loads]

    def gram_amount():
        parts = []
        for j in range(clusters):
            a_high, a_low = split(amount[GROUP * j : GROUP * j + SPAN, 0:loads])
            both = mm(gram[j], a_high)
            parts.append(both[:SPAN] + both[SPAN:] + mm(gram[j, 0:SPAN], a_low))
        rows = []
        for j in range(clusters):
            line = parts[j][GROUP : 2 * GROUP]
            if j + 1 < clusters:
                line = line + parts[j + 1][0:GROUP]
            if j > 0:
                line = line + parts[j - 1][2 * GROUP : WIDE]
            rows.append(line)
        return jnp.concatenate(rows, axis=0)

    def restrict(high, low, v):
        rows = high.shape[0]
        v_high, v_low = split(v)
        both = nt(jnp.concatenate([high, low], axis=0), v_high)
        return both[:rows] + both[rows:] + nt(high, v_low)

    def expand(amounts, rows):
        a_high, a_low = split(amounts.T)
        both = mm(jnp.concatenate([a_high, a_low], axis=0), span_h[0:rows])
        return both[:loads] + both[loads:] + mm(a_high, span_l[0:rows])

    def row_sum(v):
        part = v[:, 0:LANES]
        for t in range(1, chunks):
            part = part + v[:, t * LANES : (t + 1) * LANES]
        return jnp.sum(part.T, axis=0, keepdims=True)

    def spread(line):
        column = jnp.broadcast_to(line, (LANES, loads)).T
        return jnp.concatenate([column] * chunks, axis=1)

    low_weight = jnp.where(has_prev, 0.5, 1.0).astype(F32)
    high_weight = jnp.where(has_next, 0.5, 1.0).astype(F32)

    def weighted(v):
        return jnp.concatenate([v[:, 0:face] * low_weight, v[:, face:slots] * high_weight], axis=1)

    def assembled(k, v):
        return jnp.concatenate([v[:, 0:face] + halo[k, 0], v[:, face:slots] + halo[k, 1]], axis=1)

    def precondition(v, out, parts=2):
        rows = v.shape[0]
        pair = jnp.concatenate(split(v)[:parts], axis=0)
        for n in range(nblock):
            cols = slice(n * block, (n + 1) * block)
            weight = low_weight if n < nblock // 2 else high_weight
            both = mm(pair[:, cols], blocks[n])
            if parts == 2:
                both = both[:rows] + both[rows:]
            out[:, cols] = (weight * weight) * both

    def permute(src, order, dst, span=range(chunks)):
        rows = src.shape[0]
        for t in span:
            cols = slice(t * LANES, (t + 1) * LANES)
            line = jnp.broadcast_to(order[0:1, cols], (rows, LANES))
            lane, chunk = line & (LANES - 1), line >> 7
            found = jnp.zeros((rows, LANES), F32)
            for u in range(chunks):
                seen = jnp.take_along_axis(
                    src[:, u * LANES : (u + 1) * LANES], lane, axis=1, mode="promise_in_bounds"
                )
                found = jnp.where(chunk == u, seen, found)
            dst[:, cols] = found

    def apply(src, dst, parts):
        total = None
        step = 2 * LANES
        for t in range(slots // step):
            cols = slice(t * step, (t + 1) * step)
            permute(src, inverse, dst, range(2 * t, 2 * t + 2))
            pieces = jnp.concatenate(split(dst[:, cols])[:parts], axis=0)
            part = mm(pieces, oper[cols, :])
            total = part if total is None else total + part
        if parts == 2:
            total = total[:loads] + total[loads:]
        return softness * total

    softness = 1.0 / jnp.broadcast_to(stiff_ref[...], (loads, LANES))
    softness = jnp.concatenate([softness] * chunks, axis=1)

    def nothing():
        pass

    start_faces(basis_args)
    start_faces(halo_args[0])

    zero_tile = jnp.zeros((WIDE, LANES), F32)
    for k in range(SUMS):
        ybuf[k, y] = zero_tile
        for core_id in range(CORES):
            zbuf[k, 0, core_id] = zero_tile
            zbuf[k, nz + 1, core_id] = zero_tile
    amount[...] = jnp.zeros_like(amount)

    @pl.when(jnp.logical_not(has_prev))
    def _():
        nbr_basis[0] = jnp.zeros((GROUP, face), F32)
        halo_span[0] = jnp.zeros((SPAN, face), F32)
        for k in range(HALOS):
            halo[k, 0] = jnp.zeros((loads, face), F32)

    @pl.when(jnp.logical_not(has_next))
    def _():
        nbr_basis[1] = jnp.zeros((GROUP, face), F32)
        halo_span[1] = jnp.zeros((SPAN, face), F32)
        for k in range(HALOS):
            halo[k, 1] = jnp.zeros((loads, face), F32)

    coarse_size = coarse_ref.shape[0]
    total_rows = clusters * GROUP

    def placed(row, entry):
        return jnp.where((modes * (row >> 3) + (row & 7) == entry) & ((row & 7) < modes), 1.0, 0.0)

    shape = (total_rows, coarse_size)
    down = placed(lax.broadcasted_iota(jnp.int32, shape, 0), lax.broadcasted_iota(jnp.int32, shape, 1))
    shape = (coarse_size, total_rows)
    across = placed(
        lax.broadcasted_iota(jnp.int32, shape, 1), lax.broadcasted_iota(jnp.int32, shape, 0)
    )
    c_high, c_low = split(exact(exact(down, coarse_ref[...]), across))
    coarse[0:total_rows] = c_high
    coarse[total_rows:] = c_low

    def invert(t, carry):
        where = t * LANES + lax.broadcasted_iota(jnp.int32, (LANES, LANES), 0)
        found = jnp.zeros((LANES, LANES), F32)
        for u in range(chunks):
            here = (u * LANES + lax.broadcasted_iota(jnp.int32, (LANES, LANES), 1)).astype(F32)
            line = jnp.broadcast_to(index_ref[:, u * LANES : (u + 1) * LANES], (LANES, LANES))
            found = jnp.where(line == where, here, found)
        line = jnp.sum(found.T, axis=0, keepdims=True).astype(jnp.int32)
        inverse[:, pl.ds(pl.multiple_of(t * LANES, LANES), LANES)] = jnp.broadcast_to(
            line, (GROUP, LANES)
        )
        return carry

    lax.fori_loop(0, chunks, invert, 0)
    blocks_copy.wait()

    wait_faces(basis_args)
    low, high = nbr_basis[0], nbr_basis[1]
    at_first, at_last = first_m.astype(F32), last_m.astype(F32)
    span_f[...] = jnp.zeros_like(span_f)
    span_f[0:GROUP, 0:face] = low * at_first
    span_f[GROUP : 2 * GROUP, 0:face] = own_basis[:, 0:face] + low * (1.0 - at_first)
    span_f[GROUP : 2 * GROUP, face:slots] = own_basis[:, face:slots] + high * (1.0 - at_last)
    span_f[2 * GROUP : WIDE, face:slots] = high * at_last
    s_high, s_low = split(span_f[...])
    span_h[0:SPAN] = s_high
    span_l[0:SPAN] = s_low
    precondition(span_f[...], sent_span)
    own_gram = restrict(span_h[0:SPAN], span_l[0:SPAN], sent_span[...])
    permute(span_f, inverse, wide)
    s_high, s_low = split(wide[...])
    order_h[0:SPAN] = s_high
    order_l[0:SPAN] = s_low

    wait_faces(halo_args[0])
    resid[...] = assembled(0, load[...])
    precondition(resid[...], sent.at[0])

    terms = restrict(span_h[0:SPAN], span_l[0:SPAN], sent[0])
    o_high, o_low = split(jnp.concatenate([own_basis[...], jnp.zeros_like(own_basis)], axis=0))
    own_terms = restrict(o_high, o_low, resid[...])
    ybuf[0, y, 0:GROUP, :] = jnp.concatenate(
        [terms[0:GROUP], own_gram[0:GROUP], own_gram[GROUP : 2 * GROUP]], axis=1
    )
    ybuf[0, y, GROUP : 2 * GROUP, :] = jnp.concatenate(
        [terms[GROUP : 2 * GROUP], own_terms[0:GROUP]], axis=1
    )
    ybuf[0, y, 2 * GROUP : WIDE, 0:loads] = terms[2 * GROUP : WIDE]
    ybuf[0, y, 2 * GROUP : WIDE, loads : loads + SPAN] = own_gram[2 * GROUP : WIDE]

    def assemble_span():
        wait_faces(span_args)
        low, high = halo_span[0], halo_span[1]
        none = jnp.zeros((GROUP, face), F32)
        low_moved = jnp.concatenate([low[GROUP:SPAN], none], axis=0)
        high_moved = jnp.concatenate([none, high[0 : SPAN - GROUP]], axis=0)
        low = jnp.where(first_m, low_moved, low)
        high = jnp.where(last_m, high_moved, high)
        wide[:, 0:face] = sent_span[:, 0:face] + low
        wide[:, face:slots] = sent_span[:, face:slots] + high
        t_high, t_low = split(wide[...])
        span_h[SPAN : 2 * SPAN] = t_high
        span_l[SPAN : 2 * SPAN] = t_low
        permute(wide, inverse, span_f)
        t_high, t_low = split(span_f[...])
        order_h[SPAN : 2 * SPAN] = t_high
        order_l[SPAN : 2 * SPAN] = t_low

    reduce(
        0, WIDE, lambda: start_faces(span_args), lambda: start_faces(halo_args[1]), assemble_span
    )
    parts = gathered(0)
    for j in range(clusters):
        square = jnp.concatenate(
            [
                parts[j + 2, 0:GROUP, loads : loads + SPAN],
                parts[j + 2, 0:GROUP, loads + SPAN : LANES],
                parts[j + 2, 2 * GROUP : WIDE, loads : loads + SPAN],
                jnp.zeros((GROUP, SPAN), F32),
            ],
            axis=0,
        )
        g_high, g_low = split(square)
        gram[j, 0:SPAN] = g_high
        gram[j, SPAN : 2 * SPAN] = g_low
    totals = parts[2 : 2 + clusters, GROUP : 2 * GROUP, LANES - loads : LANES]
    amount_r = solve(totals.reshape(total_rows, loads))
    reduced = fold(parts)[:, 0:loads] - gram_amount()
    amount_y = solve(reduced)
    wait_faces(halo_args[1])
    search0[...] = assembled(1, sent[0]) - expand(
        jnp.concatenate([amount_y, amount_r], axis=0), 2 * SPAN
    )
    proj[...] = resid[...] - expand(amount_r, SPAN)

    oper_copy.wait()
    image0[...] = apply(search0, turned0, 1)
    terms = restrict(order_h[...], order_l[...], image0[...])
    ybuf[1, y] = jnp.concatenate([terms[0:WIDE], terms[SPAN : SPAN + WIDE]], axis=1)
    ybuf[1, y, 2 * GROUP - 2 : 2 * GROUP - 1, 0:loads] = row_sum(weighted(proj[...]) * search0[...])
    ybuf[1, y, 2 * GROUP - 1 : 2 * GROUP, 0:loads] = row_sum(turned0[...] * image0[...])
    reduce(
        1,
        WIDE,
        lambda: permute(image0, index_ref, sent.at[1]),
        lambda: start_faces(halo_args[2]),
        nothing,
    )
    parts = gathered(1)
    sums = jnp.sum(parts[2 : 2 + clusters, GROUP : 2 * GROUP, 0:loads], axis=0)
    rho0, gamma0 = sums[GROUP - 2 : GROUP - 1], sums[GROUP - 1 : GROUP]
    step0 = rho0 / gamma0
    totals = fold(parts)
    amount_r = amount_r - step0 * solve(totals[:, 0:loads])
    reduced = reduced - step0 * (totals[:, LANES - loads : LANES] - gram_amount())
    wait_faces(halo_args[2])
    image_q[...] = assembled(2, sent[1])
    resid[...] = resid[...] - spread(step0) * image_q[...]
    proj[...] = resid[...] - expand(amount_r, SPAN)
    precondition(proj[...], sent.at[2], 1)
    start_faces(halo_args[3])
    amount_y = solve(reduced)
    spread_y = expand(amount_y, SPAN)
    wait_faces(halo_args[3])
    search1[...] = assembled(3, sent[2]) - spread_y

    image1[...] = apply(search1, turned1, 2)
    ybuf[2, y, 0:1, 0:loads] = row_sum(weighted(proj[...]) * search1[...])
    ybuf[2, y, 1:2, 0:loads] = row_sum(turned1[...] * image1[...])
    ybuf[2, y, 2:3, 0:loads] = row_sum(turned1[...] * image0[...])
    reduce(
        2,
        GROUP,
        lambda: permute(image1, index_ref, sent.at[3]),
        lambda: start_faces(halo_args[4]),
        nothing,
    )
    sums = zbuf[2, 1, 0, 0:GROUP, 0:loads]
    for j in range(1, clusters):
        sums = sums + zbuf[2, 1 + j // CORES, j % CORES, 0:GROUP, 0:loads]
    rho1 = sums[0:1]
    beta = rho1 / rho0
    gamma1 = sums[1:2] + 2.0 * beta * sums[2:3] + beta * beta * gamma0
    step1 = rho1 / gamma1
    wait_faces(halo_args[4])
    beta_all, step0_all, step1_all = (spread(v)[:, 0:LANES] for v in (beta, step0, step1))
    for f in range(2):
        for t in range(chunks // 2):
            cols = slice(f * face + t * LANES, f * face + (t + 1) * LANES)
            near = slice(t * LANES, (t + 1) * LANES)
            rows = pl.ds(2 * t + f, loads, stride=chunks)
            first = search0[:, cols]
            direction = search1[:, cols] + beta_all * first
            mult_out[rows, :] = step0_all * first + step1_all * direction
            image = sent[3, :, cols] + halo[4, f, :, near] + beta_all * image_q[:, cols]
            resid_out[rows, :] = resid[:, cols] - step1_all * image

    drain_faces(basis_args)
    drain_faces(span_args)
    for k in range(HALOS):
        drain_faces(halo_args[k])
    for k in range(SUMS):
        drain(k, WIDE if k < SUMS - 1 else GROUP)


def per_device(
    dual_load, dual_operator, index_map, stiffness, coarse_basis, dirichlet_blocks, coarse_inverse
):
    loads, face = dual_load.shape[2], dual_load.shape[4]
    slots = 2 * face
    modes = coarse_basis.shape[2]
    clusters, members = lax.axis_size("cluster"), lax.axis_size("member")
    nz, ny, nx = clusters // CORES, NY, members // NY
    blocks_shape = dirichlet_blocks.shape[2:]
    vmem = pl.BlockSpec(memory_space=pltpu.VMEM)
    in_place = pl.BlockSpec(memory_space=pl.ANY)
    vector = pltpu.VMEM((loads, slots), F32)
    span = pltpu.VMEM((SPAN, slots), F32)
    spans = pltpu.VMEM((2 * SPAN, slots), BF16)
    dma = pltpu.SemaphoreType.DMA
    rows = loads * slots // LANES
    lines = (loads, face // LANES, 2, LANES)
    load = dual_load.reshape(loads, 2, face // LANES, LANES).transpose(0, 2, 1, 3)
    outs = pl.pallas_call(
        kernel,
        out_shape=[pltpu.VMEM((rows, LANES), F32)] * 2,
        in_specs=[vmem] * 4 + [in_place] * 3,
        out_specs=[vmem] * 2,
        scratch_shapes=[
            pltpu.VMEM((rows, LANES), F32),
            pltpu.VMEM(blocks_shape, BF16),
            pltpu.VMEM((slots, slots), BF16),
            vector,
            pltpu.VMEM((GROUP, slots), F32),
            pltpu.VMEM((2, GROUP, face), F32),
            span,
            spans,
            spans,
            spans,
            spans,
            span,
            pltpu.VMEM((2 * clusters * GROUP, clusters * GROUP), BF16),
            pltpu.VMEM(((clusters + 3) * GROUP, LANES), F32),
            pltpu.VMEM((clusters, 2 * SPAN, SPAN), BF16),
            pltpu.VMEM((GROUP, slots), jnp.int32),
            pltpu.VMEM((HALOS, 2, loads, face), F32),
            pltpu.VMEM((2, SPAN, face), F32),
            pltpu.VMEM((HALOS - 1, loads, slots), F32),
            span,
        ]
        + [vector] * 9
        + [
            pltpu.VMEM((SUMS, ny, WIDE, LANES), F32),
            pltpu.VMEM((SUMS, nx, WIDE, LANES), F32),
            pltpu.VMEM((SUMS, nz + 2, CORES, WIDE, LANES), F32),
            dma((3,)),
            dma((2,)),
            dma((2,)),
            dma((2,)),
            dma((2,)),
            dma((HALOS, 2)),
            dma((HALOS, 2)),
        ]
        + [dma((SUMS,))] * 8,
        compiler_params=pltpu.CompilerParams(
            collective_id=0, has_side_effects=True, vmem_limit_bytes=62 * 2**20
        ),
        name="pcpg",
    )(
        coarse_basis.reshape(modes, 1, slots),
        coarse_inverse,
        index_map.reshape(1, slots),
        stiffness,
        load.reshape(rows, LANES),
        dirichlet_blocks.reshape(blocks_shape),
        dual_operator,
    )
    mult, resid = (out.reshape(lines).transpose(0, 2, 1, 3).reshape(dual_load.shape) for out in outs)
    return mult, resid


def solution(mesh):
    five = P("cluster", "member", None, None, None)
    in_specs = (
        five,
        P(),
        P("cluster", "member", None),
        P("cluster", "member"),
        P("cluster", "member", None, None),
        five,
        P(),
    )
    return jax.shard_map(
        per_device, mesh=mesh, in_specs=in_specs, out_specs=(five, five), check_vma=False
    )
```

```python
import jax
import jax.numpy as jnp
from jax import lax
from jax.experimental import pallas as pl
from jax.experimental.pallas import tpu as pltpu
from jax.sharding import PartitionSpec as P

MESH = pl.DeviceIdType.MESH
NY = 8
CORES = 2
GROUP = 8
SPAN = 32
LANES = 128
HALOS = 5
SUMS = 3
WIDE = 3 * GROUP
F32 = jnp.float32
BF16 = jnp.bfloat16


def nt(a, b):
    return lax.dot_general(a, b, (((1,), (1,)), ((), ())), preferred_element_type=F32)


def mm(a, b):
    return jnp.dot(a, b, preferred_element_type=F32)


def exact(a, b):
    return jnp.dot(a, b, precision=lax.Precision.HIGHEST, preferred_element_type=F32)


def split(v):
    high = v.astype(BF16)
    return high, (v - high.astype(F32)).astype(BF16)


def kernel(
    stiff_ref,
    basis_hbm,
    coarse_hbm,
    index_hbm,
    load_hbm,
    blocks_hbm,
    oper_hbm,
    mult_out,
    resid_out,
    basis_ref,
    coarse_ref,
    index_ref,
    raw,
    blocks,
    oper,
    load,
    own_basis,
    nbr_basis,
    span_f,
    span_h,
    span_l,
    order_h,
    order_l,
    wide,
    coarse,
    amount,
    gram,
    inverse,
    halo,
    halo_span,
    sent,
    sent_span,
    resid,
    proj,
    search0,
    search1,
    image_q,
    turned0,
    turned1,
    image0,
    image1,
    ybuf,
    xbuf,
    zbuf,
    local_sem,
    basis_s,
    basis_r,
    span_s,
    span_r,
    halo_s,
    halo_r,
    y_s,
    y_r,
    x_s,
    x_r,
    z_s,
    z_r,
    c_s,
    c_r,
):
    loads, slots = load.shape
    face = slots // 2
    chunks = slots // LANES
    modes = basis_ref.shape[0]
    nblock, block = blocks.shape[:2]
    nz = zbuf.shape[1] - 2
    nx = xbuf.shape[1]
    ny = ybuf.shape[1]
    members = nx * ny
    clusters = nz * CORES
    c = lax.axis_index("cluster")
    m = lax.axis_index("member")
    z, core = c // CORES, lax.rem(c, CORES)
    x, y = m // ny, lax.rem(m, ny)
    chain = c * members + m
    last = clusters * members - 1
    has_prev, has_next = chain > 0, chain < last
    first_m, last_m = m == 0, m == members - 1
    prev = (jnp.where(first_m, c - 1, c), jnp.where(first_m, members - 1, m - 1))
    nxt = (jnp.where(last_m, c + 1, c), jnp.where(last_m, 0, m + 1))

    def far_first(count):
        return sorted(range(1, count), key=lambda i: -min(i, count - i))

    y_peers = [(c, x * ny + lax.rem(y + i, ny)) for i in far_first(ny)]
    x_peers = [(c, lax.rem(x + i, nx) * ny + y) for i in far_first(nx)]
    z_peers = [(lax.rem(z + i, nz) * CORES + core, m) for i in far_first(nz)]
    partner = (z * CORES + 1 - core, m)

    def copy(src, dst, ss, rs, device):
        return pltpu.make_async_remote_copy(
            src_ref=src, dst_ref=dst, send_sem=ss, recv_sem=rs, device_id=device, device_id_type=MESH
        )

    def take(ref, sem):
        pltpu.make_async_copy(ref, ref, sem).wait()

    barrier = pltpu.get_barrier_semaphore()
    peers = z_peers + y_peers + x_peers + [partner]
    for peer in peers:
        pl.semaphore_signal(barrier, inc=1, device_id=peer, device_id_type=MESH)

    @pl.when(has_prev)
    def _():
        pl.semaphore_signal(barrier, inc=1, device_id=prev, device_id_type=MESH)

    @pl.when(has_next)
    def _():
        pl.semaphore_signal(barrier, inc=1, device_id=nxt, device_id_type=MESH)

    raw_copy = pltpu.make_async_copy(load_hbm, raw, local_sem.at[0])
    blocks_copy = pltpu.make_async_copy(blocks_hbm, blocks, local_sem.at[1])
    oper_copy = pltpu.make_async_copy(oper_hbm, oper, local_sem.at[2])
    basis_copy = pltpu.make_async_copy(basis_hbm, basis_ref, local_sem.at[3])
    coarse_copy = pltpu.make_async_copy(coarse_hbm, coarse_ref, local_sem.at[4])
    index_copy = pltpu.make_async_copy(index_hbm, index_ref, local_sem.at[5])
    for each in (basis_copy, raw_copy, coarse_copy, index_copy, blocks_copy, oper_copy):
        each.start()

    own_basis[...] = jnp.zeros_like(own_basis)
    basis_copy.wait()
    for k in range(modes):
        own_basis[k : k + 1, :] = basis_ref[k]
    raw_copy.wait()
    for f in range(2):
        for t in range(chunks // 2):
            start = f * face + t * LANES
            load[:, start : start + LANES] = raw[pl.ds(2 * t + f, loads, stride=chunks), :]

    greetings = len(peers) + has_prev.astype(jnp.int32) + has_next.astype(jnp.int32)
    pl.semaphore_wait(barrier, greetings)

    def faces(src, dst, ss, rs):
        up = copy(src.at[:, pl.ds(face, face)], dst.at[0], ss.at[0], rs.at[0], nxt)
        down = copy(src.at[:, pl.ds(0, face)], dst.at[1], ss.at[1], rs.at[1], prev)
        return up, down

    def start_faces(args):
        up, down = faces(*args)

        @pl.when(has_next)
        def _():
            up.start()

        @pl.when(has_prev)
        def _():
            down.start()

    def wait_faces(args):
        up, down = faces(*args)

        @pl.when(has_prev)
        def _():
            up.wait_recv()

        @pl.when(has_next)
        def _():
            down.wait_recv()

    def drain_faces(args):
        up, down = faces(*args)

        @pl.when(has_next)
        def _():
            up.wait_send()

        @pl.when(has_prev)
        def _():
            down.wait_send()

    basis_args = (own_basis, nbr_basis, basis_s, basis_r)
    span_args = (sent_span, halo_span, span_s, span_r)
    halo_args = [
        (load if k == 0 else sent.at[k - 1], halo.at[k], halo_s.at[k], halo_r.at[k])
        for k in range(HALOS)
    ]

    def reduce(k, rows, after_y, after_x, after_z):
        own = ybuf.at[k, y, 0:rows]
        for peer in y_peers:
            copy(own, own, y_s.at[k], y_r.at[k], peer).start()
        after_y()
        take(ybuf.at[k, 0 : ny - 1, 0:rows], y_r.at[k])
        total = ybuf[k, 0, 0:rows]
        for i in range(1, ny):
            total = total + ybuf[k, i, 0:rows]
        xbuf[k, x, 0:rows] = total
        own = xbuf.at[k, x, 0:rows]
        for peer in x_peers:
            copy(own, own, x_s.at[k], x_r.at[k], peer).start()
        after_x()
        take(xbuf.at[k, 0 : nx - 1, 0:rows], x_r.at[k])
        total = xbuf[k, 0, 0:rows]
        for i in range(1, nx):
            total = total + xbuf[k, i, 0:rows]
        zbuf[k, z + 1, core, 0:rows] = total
        own = zbuf.at[k, z + 1, core, 0:rows]
        for peer in z_peers:
            copy(own, own, z_s.at[k], z_r.at[k], peer).start()
        after_z()
        take(zbuf.at[k, 1:nz, 0, 0:rows], z_r.at[k])
        mine = zbuf.at[k, 1 : nz + 1, core, 0:rows]
        swap = copy(mine, mine, c_s.at[k], c_r.at[k], partner)
        swap.start()
        swap.wait_recv()

    def drain(k, rows):
        take(ybuf.at[k, 0 : ny - 1, 0:rows], y_s.at[k])
        take(xbuf.at[k, 0 : nx - 1, 0:rows], x_s.at[k])
        take(zbuf.at[k, 1:nz, 0, 0:rows], z_s.at[k])
        take(zbuf.at[k, 1 : nz + 1, 0, 0:rows], c_s.at[k])

    def gathered(k):
        return zbuf[k].reshape(CORES * (nz + 2), WIDE, LANES)

    def fold(parts):
        total = (
            parts[2 : 2 + clusters, GROUP : 2 * GROUP]
            + parts[3 : 3 + clusters, 0:GROUP]
            + parts[1 : 1 + clusters, 2 * GROUP : WIDE]
        )
        return total.reshape(total_rows, LANES)

    def solve(totals):
        t_high, t_low = split(totals)
        both = mm(coarse[...], t_high)
        amounts = both[:total_rows] + both[total_rows:] + mm(coarse[0:total_rows], t_low)
        amount[GROUP : GROUP + total_rows, 0:loads] = amounts
        return amount[pl.ds(pl.multiple_of(GROUP * c, GROUP), SPAN), 0:loads]

    def gram_amount():
        parts = []
        for j in range(clusters):
            a_high, a_low = split(amount[GROUP * j : GROUP * j + SPAN, 0:loads])
            both = mm(gram[j], a_high)
            parts.append(both[:SPAN] + both[SPAN:] + mm(gram[j, 0:SPAN], a_low))
        rows = []
        for j in range(clusters):
            line = parts[j][GROUP : 2 * GROUP]
            if j + 1 < clusters:
                line = line + parts[j + 1][0:GROUP]
            if j > 0:
                line = line + parts[j - 1][2 * GROUP : WIDE]
            rows.append(line)
        return jnp.concatenate(rows, axis=0)

    def restrict(high, low, v):
        rows = high.shape[0]
        v_high, v_low = split(v)
        both = nt(jnp.concatenate([high, low], axis=0), v_high)
        return both[:rows] + both[rows:] + nt(high, v_low)

    def expand(amounts, rows):
        a_high, a_low = split(amounts.T)
        both = mm(jnp.concatenate([a_high, a_low], axis=0), span_h[0:rows])
        return both[:loads] + both[loads:] + mm(a_high, span_l[0:rows])

    def row_sum(v):
        part = v[:, 0:LANES]
        for t in range(1, chunks):
            part = part + v[:, t * LANES : (t + 1) * LANES]
        return jnp.sum(part.T, axis=0, keepdims=True)

    def spread(line):
        column = jnp.broadcast_to(line, (LANES, loads)).T
        return jnp.concatenate([column] * chunks, axis=1)

    low_weight = jnp.where(has_prev, 0.5, 1.0).astype(F32)
    high_weight = jnp.where(has_next, 0.5, 1.0).astype(F32)

    def weighted(v):
        return jnp.concatenate([v[:, 0:face] * low_weight, v[:, face:slots] * high_weight], axis=1)

    def assembled(k, v):
        return jnp.concatenate([v[:, 0:face] + halo[k, 0], v[:, face:slots] + halo[k, 1]], axis=1)

    def precondition(v, out, parts=2):
        rows = v.shape[0]
        pair = jnp.concatenate(split(v)[:parts], axis=0)
        for n in range(nblock):
            cols = slice(n * block, (n + 1) * block)
            weight = low_weight if n < nblock // 2 else high_weight
            both = mm(pair[:, cols], blocks[n])
            if parts == 2:
                both = both[:rows] + both[rows:]
            out[:, cols] = (weight * weight) * both

    def permute(src, order, dst, span=range(chunks)):
        rows = src.shape[0]
        for t in span:
            cols = slice(t * LANES, (t + 1) * LANES)
            line = jnp.broadcast_to(order[0:1, cols], (rows, LANES))
            lane, chunk = line & (LANES - 1), line >> 7
            found = jnp.zeros((rows, LANES), F32)
            for u in range(chunks):
                seen = jnp.take_along_axis(
                    src[:, u * LANES : (u + 1) * LANES], lane, axis=1, mode="promise_in_bounds"
                )
                found = jnp.where(chunk == u, seen, found)
            dst[:, cols] = found

    def apply(src, dst, parts):
        total = None
        step = 2 * LANES
        for t in range(slots // step):
            cols = slice(t * step, (t + 1) * step)
            permute(src, inverse, dst, range(2 * t, 2 * t + 2))
            pieces = jnp.concatenate(split(dst[:, cols])[:parts], axis=0)
            part = mm(pieces, oper[cols, :])
            total = part if total is None else total + part
        if parts == 2:
            total = total[:loads] + total[loads:]
        return softness * total

    softness = 1.0 / jnp.broadcast_to(stiff_ref[...], (loads, LANES))
    softness = jnp.concatenate([softness] * chunks, axis=1)

    def nothing():
        pass

    start_faces(basis_args)
    start_faces(halo_args[0])

    zero_tile = jnp.zeros((WIDE, LANES), F32)
    for k in range(SUMS):
        ybuf[k, y] = zero_tile
        for core_id in range(CORES):
            zbuf[k, 0, core_id] = zero_tile
            zbuf[k, nz + 1, core_id] = zero_tile
    amount[...] = jnp.zeros_like(amount)

    @pl.when(jnp.logical_not(has_prev))
    def _():
        nbr_basis[0] = jnp.zeros((GROUP, face), F32)
        halo_span[0] = jnp.zeros((SPAN, face), F32)
        for k in range(HALOS):
            halo[k, 0] = jnp.zeros((loads, face), F32)

    @pl.when(jnp.logical_not(has_next))
    def _():
        nbr_basis[1] = jnp.zeros((GROUP, face), F32)
        halo_span[1] = jnp.zeros((SPAN, face), F32)
        for k in range(HALOS):
            halo[k, 1] = jnp.zeros((loads, face), F32)

    coarse_copy.wait()
    index_copy.wait()
    coarse_size = coarse_ref.shape[0]
    total_rows = clusters * GROUP

    def placed(row, entry):
        return jnp.where((modes * (row >> 3) + (row & 7) == entry) & ((row & 7) < modes), 1.0, 0.0)

    shape = (total_rows, coarse_size)
    down = placed(lax.broadcasted_iota(jnp.int32, shape, 0), lax.broadcasted_iota(jnp.int32, shape, 1))
    shape = (coarse_size, total_rows)
    across = placed(
        lax.broadcasted_iota(jnp.int32, shape, 1), lax.broadcasted_iota(jnp.int32, shape, 0)
    )
    c_high, c_low = split(exact(exact(down, coarse_ref[...]), across))
    coarse[0:total_rows] = c_high
    coarse[total_rows:] = c_low

    def invert(t, carry):
        where = t * LANES + lax.broadcasted_iota(jnp.int32, (LANES, LANES), 0)
        found = jnp.zeros((LANES, LANES), F32)
        for u in range(chunks):
            here = (u * LANES + lax.broadcasted_iota(jnp.int32, (LANES, LANES), 1)).astype(F32)
            line = jnp.broadcast_to(index_ref[:, u * LANES : (u + 1) * LANES], (LANES, LANES))
            found = jnp.where(line == where, here, found)
        line = jnp.sum(found.T, axis=0, keepdims=True).astype(jnp.int32)
        inverse[:, pl.ds(pl.multiple_of(t * LANES, LANES), LANES)] = jnp.broadcast_to(
            line, (GROUP, LANES)
        )
        return carry

    lax.fori_loop(0, chunks, invert, 0)
    blocks_copy.wait()

    wait_faces(basis_args)
    low, high = nbr_basis[0], nbr_basis[1]
    at_first, at_last = first_m.astype(F32), last_m.astype(F32)
    span_f[...] = jnp.zeros_like(span_f)
    span_f[0:GROUP, 0:face] = low * at_first
    span_f[GROUP : 2 * GROUP, 0:face] = own_basis[:, 0:face] + low * (1.0 - at_first)
    span_f[GROUP : 2 * GROUP, face:slots] = own_basis[:, face:slots] + high * (1.0 - at_last)
    span_f[2 * GROUP : WIDE, face:slots] = high * at_last
    s_high, s_low = split(span_f[...])
    span_h[0:SPAN] = s_high
    span_l[0:SPAN] = s_low
    precondition(span_f[...], sent_span)
    own_gram = restrict(span_h[0:SPAN], span_l[0:SPAN], sent_span[...])
    permute(span_f, inverse, wide)
    s_high, s_low = split(wide[...])
    order_h[0:SPAN] = s_high
    order_l[0:SPAN] = s_low

    wait_faces(halo_args[0])
    resid[...] = assembled(0, load[...])
    precondition(resid[...], sent.at[0])

    terms = restrict(span_h[0:SPAN], span_l[0:SPAN], sent[0])
    o_high, o_low = split(jnp.concatenate([own_basis[...], jnp.zeros_like(own_basis)], axis=0))
    own_terms = restrict(o_high, o_low, resid[...])
    ybuf[0, y, 0:GROUP, :] = jnp.concatenate(
        [terms[0:GROUP], own_gram[0:GROUP], own_gram[GROUP : 2 * GROUP]], axis=1
    )
    ybuf[0, y, GROUP : 2 * GROUP, :] = jnp.concatenate(
        [terms[GROUP : 2 * GROUP], own_terms[0:GROUP]], axis=1
    )
    ybuf[0, y, 2 * GROUP : WIDE, 0:loads] = terms[2 * GROUP : WIDE]
    ybuf[0, y, 2 * GROUP : WIDE, loads : loads + SPAN] = own_gram[2 * GROUP : WIDE]

    def assemble_span():
        wait_faces(span_args)
        low, high = halo_span[0], halo_span[1]
        none = jnp.zeros((GROUP, face), F32)
        low_moved = jnp.concatenate([low[GROUP:SPAN], none], axis=0)
        high_moved = jnp.concatenate([none, high[0 : SPAN - GROUP]], axis=0)
        low = jnp.where(first_m, low_moved, low)
        high = jnp.where(last_m, high_moved, high)
        wide[:, 0:face] = sent_span[:, 0:face] + low
        wide[:, face:slots] = sent_span[:, face:slots] + high
        t_high, t_low = split(wide[...])
        span_h[SPAN : 2 * SPAN] = t_high
        span_l[SPAN : 2 * SPAN] = t_low
        permute(wide, inverse, span_f)
        t_high, t_low = split(span_f[...])
        order_h[SPAN : 2 * SPAN] = t_high
        order_l[SPAN : 2 * SPAN] = t_low

    reduce(
        0, WIDE, lambda: start_faces(span_args), lambda: start_faces(halo_args[1]), assemble_span
    )
    parts = gathered(0)
    for j in range(clusters):
        square = jnp.concatenate(
            [
                parts[j + 2, 0:GROUP, loads : loads + SPAN],
                parts[j + 2, 0:GROUP, loads + SPAN : LANES],
                parts[j + 2, 2 * GROUP : WIDE, loads : loads + SPAN],
                jnp.zeros((GROUP, SPAN), F32),
            ],
            axis=0,
        )
        g_high, g_low = split(square)
        gram[j, 0:SPAN] = g_high
        gram[j, SPAN : 2 * SPAN] = g_low
    totals = parts[2 : 2 + clusters, GROUP : 2 * GROUP, LANES - loads : LANES]
    amount_r = solve(totals.reshape(total_rows, loads))
    reduced = fold(parts)[:, 0:loads] - gram_amount()
    amount_y = solve(reduced)
    wait_faces(halo_args[1])
    search0[...] = assembled(1, sent[0]) - expand(
        jnp.concatenate([amount_y, amount_r], axis=0), 2 * SPAN
    )
    proj[...] = resid[...] - expand(amount_r, SPAN)

    oper_copy.wait()
    image0[...] = apply(search0, turned0, 1)
    terms = restrict(order_h[...], order_l[...], image0[...])
    ybuf[1, y] = jnp.concatenate([terms[0:WIDE], terms[SPAN : SPAN + WIDE]], axis=1)
    ybuf[1, y, 2 * GROUP - 2 : 2 * GROUP - 1, 0:loads] = row_sum(weighted(proj[...]) * search0[...])
    ybuf[1, y, 2 * GROUP - 1 : 2 * GROUP, 0:loads] = row_sum(turned0[...] * image0[...])
    reduce(
        1,
        WIDE,
        lambda: permute(image0, index_ref, sent.at[1]),
        lambda: start_faces(halo_args[2]),
        nothing,
    )
    parts = gathered(1)
    sums = jnp.sum(parts[2 : 2 + clusters, GROUP : 2 * GROUP, 0:loads], axis=0)
    rho0, gamma0 = sums[GROUP - 2 : GROUP - 1], sums[GROUP - 1 : GROUP]
    step0 = rho0 / gamma0
    totals = fold(parts)
    amount_r = amount_r - step0 * solve(totals[:, 0:loads])
    reduced = reduced - step0 * (totals[:, LANES - loads : LANES] - gram_amount())
    wait_faces(halo_args[2])
    image_q[...] = assembled(2, sent[1])
    resid[...] = resid[...] - spread(step0) * image_q[...]
    proj[...] = resid[...] - expand(amount_r, SPAN)
    precondition(proj[...], sent.at[2], 1)
    start_faces(halo_args[3])
    amount_y = solve(reduced)
    spread_y = expand(amount_y, SPAN)
    wait_faces(halo_args[3])
    search1[...] = assembled(3, sent[2]) - spread_y

    image1[...] = apply(search1, turned1, 2)
    ybuf[2, y, 0:1, 0:loads] = row_sum(weighted(proj[...]) * search1[...])
    ybuf[2, y, 1:2, 0:loads] = row_sum(turned1[...] * image1[...])
    ybuf[2, y, 2:3, 0:loads] = row_sum(turned1[...] * image0[...])
    reduce(
        2,
        GROUP,
        lambda: permute(image1, index_ref, sent.at[3]),
        lambda: start_faces(halo_args[4]),
        nothing,
    )
    sums = zbuf[2, 1, 0, 0:GROUP, 0:loads]
    for j in range(1, clusters):
        sums = sums + zbuf[2, 1 + j // CORES, j % CORES, 0:GROUP, 0:loads]
    rho1 = sums[0:1]
    beta = rho1 / rho0
    gamma1 = sums[1:2] + 2.0 * beta * sums[2:3] + beta * beta * gamma0
    step1 = rho1 / gamma1
    wait_faces(halo_args[4])
    beta_all, step0_all, step1_all = (spread(v)[:, 0:LANES] for v in (beta, step0, step1))
    for f in range(2):
        for t in range(chunks // 2):
            cols = slice(f * face + t * LANES, f * face + (t + 1) * LANES)
            near = slice(t * LANES, (t + 1) * LANES)
            rows = pl.ds(2 * t + f, loads, stride=chunks)
            first = search0[:, cols]
            direction = search1[:, cols] + beta_all * first
            mult_out[rows, :] = step0_all * first + step1_all * direction
            image = sent[3, :, cols] + halo[4, f, :, near] + beta_all * image_q[:, cols]
            resid_out[rows, :] = resid[:, cols] - step1_all * image

    drain_faces(basis_args)
    drain_faces(span_args)
    for k in range(HALOS):
        drain_faces(halo_args[k])
    for k in range(SUMS):
        drain(k, WIDE if k < SUMS - 1 else GROUP)


def per_device(
    dual_load, dual_operator, index_map, stiffness, coarse_basis, dirichlet_blocks, coarse_inverse
):
    loads, face = dual_load.shape[2], dual_load.shape[4]
    slots = 2 * face
    modes = coarse_basis.shape[2]
    clusters, members = lax.axis_size("cluster"), lax.axis_size("member")
    nz, ny, nx = clusters // CORES, NY, members // NY
    blocks_shape = dirichlet_blocks.shape[2:]
    vmem = pl.BlockSpec(memory_space=pltpu.VMEM)
    in_place = pl.BlockSpec(memory_space=pl.ANY)
    vector = pltpu.VMEM((loads, slots), F32)
    span = pltpu.VMEM((SPAN, slots), F32)
    spans = pltpu.VMEM((2 * SPAN, slots), BF16)
    dma = pltpu.SemaphoreType.DMA
    rows = loads * slots // LANES
    lines = (loads, face // LANES, 2, LANES)
    load = dual_load.reshape(loads, 2, face // LANES, LANES).transpose(0, 2, 1, 3)
    outs = pl.pallas_call(
        kernel,
        out_shape=[pltpu.VMEM((rows, LANES), F32)] * 2,
        in_specs=[vmem] + [in_place] * 6,
        out_specs=[vmem] * 2,
        scratch_shapes=[
            pltpu.VMEM((modes, 1, slots), F32),
            pltpu.VMEM(coarse_inverse.shape, F32),
            pltpu.VMEM((1, slots), jnp.int32),
            pltpu.VMEM((rows, LANES), F32),
            pltpu.VMEM(blocks_shape, BF16),
            pltpu.VMEM((slots, slots), BF16),
            vector,
            pltpu.VMEM((GROUP, slots), F32),
            pltpu.VMEM((2, GROUP, face), F32),
            span,
            spans,
            spans,
            spans,
            spans,
            span,
            pltpu.VMEM((2 * clusters * GROUP, clusters * GROUP), BF16),
            pltpu.VMEM(((clusters + 3) * GROUP, LANES), F32),
            pltpu.VMEM((clusters, 2 * SPAN, SPAN), BF16),
            pltpu.VMEM((GROUP, slots), jnp.int32),
            pltpu.VMEM((HALOS, 2, loads, face), F32),
            pltpu.VMEM((2, SPAN, face), F32),
            pltpu.VMEM((HALOS - 1, loads, slots), F32),
            span,
        ]
        + [vector] * 9
        + [
            pltpu.VMEM((SUMS, ny, WIDE, LANES), F32),
            pltpu.VMEM((SUMS, nx, WIDE, LANES), F32),
            pltpu.VMEM((SUMS, nz + 2, CORES, WIDE, LANES), F32),
            dma((6,)),
            dma((2,)),
            dma((2,)),
            dma((2,)),
            dma((2,)),
            dma((HALOS, 2)),
            dma((HALOS, 2)),
        ]
        + [dma((SUMS,))] * 8,
        compiler_params=pltpu.CompilerParams(
            collective_id=0, has_side_effects=True, vmem_limit_bytes=62 * 2**20
        ),
        name="pcpg",
    )(
        stiffness,
        coarse_basis.reshape(modes, 1, slots),
        coarse_inverse,
        index_map.reshape(1, slots),
        load.reshape(rows, LANES),
        dirichlet_blocks.reshape(blocks_shape),
        dual_operator,
    )
    mult, resid = (out.reshape(lines).transpose(0, 2, 1, 3).reshape(dual_load.shape) for out in outs)
    return mult, resid


def solution(mesh):
    five = P("cluster", "member", None, None, None)
    in_specs = (
        five,
        P(),
        P("cluster", "member", None),
        P("cluster", "member"),
        P("cluster", "member", None, None),
        five,
        P(),
    )
    return jax.shard_map(
        per_device, mesh=mesh, in_specs=in_specs, out_specs=(five, five), check_vma=False
    )
```
